1024 devices in a mesh: ctx: 64 (over z, core), head: 16 (over x, y).
Axes of the slice: x: 4, y: 4, z: 32, core: 2. Of those that a mesh axis runs over, the one named last changes fastest.
Arguments:
- hidden: bfloat16 [16384, 2048], P('ctx'), may hold values from -6 to 6
- w_query: bfloat16 [2048, 2048], P('head'), may hold values from -0.125 to 0.125
- w_key: bfloat16 [2048, 2048], P('head'), may hold values from -0.125 to 0.125
- payload_projection_matrix: bfloat16 [2048, 4096], P('head'), may hold values from -0.125 to 0.125
- conv_weight: bfloat16 [4, 8192], replicated, may hold values from -3 to 3
- log_decay: float32 [32, 16384], P('head', 'ctx'), may hold values from -1.6 to 0
- beta_rate: float32 [32, 16384], P('head', 'ctx'), may hold values from 0 to 1
- norm_gain: float32 [128], replicated, may hold values from 0.25 to 1.75
- head_order: int32 [16], replicated, may hold values from 0 to 15, each once
- block_starts: int32 [64], P('ctx'), may hold values 0 or 1
Outputs:
- mixed: bfloat16 [16384, 4096], P('ctx', 'head')
The draws below stay inside these ranges and needn't reach their ends.
Inputs may be any that keep to these rules, and one draw needn't show every extreme that they name: Index j of the head axis serves serving key head j (logical key head head_order[j]) and serving value heads 2j and 2j + 1.
All inputs are finite; a program needn't handle non-finite values. No bound on the sum of `block_starts` on one device may be relied on, other than what follows from the above.
Results may differ from the reference program's by a relative error of at most 0.0046.
Values may be sent and summed in bfloat16 or wider, within the bound.
A program may use at most 64 MiB of HBM per device.

```python
import math
import jax
import jax.numpy as jnp
from jax import lax

D = 2048
HK = 16
VH = 32
DK = 128
VALUE_HEAD_SIZE = 128
KCONV = 4
GROUP = 64
TOK_DEV = 256
TOKENS = 16384
BLOCKS = 64


def head_speed(key):
    picks = jax.random.uniform(jax.random.fold_in(key, 101), (VH,), jnp.float32)
    share = 0.5
    return picks < share


def draw_log_decay(key, part):
    fast = head_speed(key)
    keys = jax.random.split(jax.random.fold_in(key, 7), 6)
    quick = jnp.exp(jax.random.uniform(keys[0], (VH,), jnp.float32, math.log(1.0 / 60.0), math.log(1.0 / 15.0)))
    lasting = jnp.exp(jax.random.uniform(keys[1], (VH,), jnp.float32, math.log(0.05), math.log(0.2))) / TOKENS
    base = jnp.where(fast, quick, lasting)
    per_block = jnp.exp(jax.random.uniform(keys[2], (VH, TOKENS // TOK_DEV), jnp.float32, math.log(0.5), math.log(2.0)))
    rough = jax.random.uniform(keys[3], (VH, TOKENS), jnp.float32, 0.5, 1.5)
    delta_writing_strength = base[:, None] * jnp.repeat(per_block, TOK_DEV, axis=1) * rough
    destination_slots = jax.random.randint(keys[4], (VH, 2), 0, TOKENS)
    forgetting_amounts = jax.random.uniform(keys[5], (VH, 2), jnp.float32, 0.2, 0.5)
    attention_lane_sites = jnp.arange(TOKENS)[None, None, :]
    forgetting_spike_multiplier = jnp.sum(jnp.where(attention_lane_sites == destination_slots[:, :, None], jnp.log(1.0 - forgetting_amounts)[:, :, None], 0.0), axis=1)
    return (forgetting_spike_multiplier - delta_writing_strength).astype(jnp.float32)


def draw_beta_rate(key, part):
    fast = head_speed(key)
    keys = jax.random.split(jax.random.fold_in(key, 13), 3)
    quick = jax.random.uniform(keys[0], (VH, TOKENS), jnp.float32, 0.2, 0.9)
    level = jnp.exp(jax.random.uniform(keys[1], (VH,), jnp.float32, math.log(0.2), math.log(0.8))) * DK / TOKENS
    slow = level[:, None] * jax.random.uniform(keys[2], (VH, TOKENS), jnp.float32, 0.5, 1.5)
    return jnp.where(fast[:, None], quick, slow).astype(jnp.float32)


def with_ends(values, own_key, least, largest):
    spot = [jax.random.randint(jax.random.fold_in(own_key, axis), (), 0, length) for axis, length in enumerate(values.shape)]
    longest = values.shape.index(max(values.shape))
    neighbour = spot[:longest] + [(spot[longest] + 1) % values.shape[longest]] + spot[longest + 1:]
    return values.at[tuple(spot)].set(least).at[tuple(neighbour)].set(largest)


def steps_of(key, shape, cuts, least, largest):
    level, own = 1.0, jax.random.fold_in(key, 6)
    for axis_at, blocks in cuts:
        draws = jnp.exp(jax.random.uniform(jax.random.fold_in(own, axis_at), (blocks,), jnp.float32, least / len(cuts), largest / len(cuts)))
        level = level * jnp.repeat(draws, shape[axis_at] // blocks).reshape([-1 if axis == axis_at else 1 for axis in range(len(shape))])
    return level


def normal_values(rng, extent, width, limit, shards=(), kind=jnp.bfloat16):
    drawn = jax.random.normal(rng, extent, jnp.float32) * width
    if len(shards) > 0:
        drawn = steps_of(rng, extent, shards, -0.22, 0.18) * drawn
    return jnp.clip(drawn, min=-limit, max=limit).astype(kind)


def setup_inputs(seed: int = 0) -> dict:
    arg_keys = jax.random.split(jax.random.key(seed), 11)
    return {
        "hidden": normal_values(arg_keys[0], (TOKENS, D), 1.0, 6.0, ((0, 64),)),
        "w_query": normal_values(arg_keys[1], (D, HK * DK), D ** -0.5, 0.125, ((0, 16),)),
        "w_key": normal_values(arg_keys[2], (D, HK * DK), D ** -0.5, 0.125, ((0, 16),)),
        "payload_projection_matrix": normal_values(arg_keys[3], (D, VH * VALUE_HEAD_SIZE), D ** -0.5, 0.125, ((0, 16),)),
        "conv_weight": normal_values(arg_keys[4], (KCONV, 2 * HK * DK + VH * VALUE_HEAD_SIZE), KCONV ** -0.5, 3.0),
        "log_decay": draw_log_decay(jax.random.fold_in(arg_keys[10], 71), 0),
        "beta_rate": draw_beta_rate(jax.random.fold_in(arg_keys[10], 71), 0),
        "norm_gain": jnp.clip(1.0 + 0.15 * jax.random.normal(arg_keys[7], (VALUE_HEAD_SIZE,), jnp.float32), 0.25, 1.75),
        "head_order": jax.random.permutation(arg_keys[8], HK).astype(jnp.int32),
        "block_starts": with_ends((jax.random.randint(arg_keys[9], (BLOCKS,), 0, 8) < 1).astype(jnp.int32), jax.random.fold_in(arg_keys[9], 1), 0, 1),
    }


HIGH_PRECISION = lax.Precision.HIGHEST
eps = 1e-06

def lower_solve(system, right):
    return lax.linalg.triangular_solve(system, right, left_side=True, lower=True, unit_diagonal=True)

def unit_rows(values):
    return values * lax.rsqrt(lax.optimization_barrier(jnp.sum(values * values, axis=-1, keepdims=True)) + eps)

def group_step(running_state, inputs):
    query_vector, key_vec, value, decay, delta_writing_strength, keep = inputs
    running_state = running_state * keep
    size_c = decay.shape[-1]
    cumulative_decay = jnp.cumsum(decay, axis=-1)
    rows = lax.broadcasted_iota(jnp.int32, (size_c, size_c), 0)
    cols = lax.broadcasted_iota(jnp.int32, (size_c, size_c), 1)
    spread = cumulative_decay[:, :, None] - cumulative_decay[:, None, :]
    strict_w = jnp.where(cols < rows, jnp.exp(jnp.where(cols < rows, spread, 0.0)), 0.0)
    incl_w = jnp.where(cols <= rows, jnp.exp(jnp.where(cols <= rows, spread, 0.0)), 0.0)
    key_key = jnp.einsum('htd,hsd->hts', key_vec, key_vec, precision=HIGH_PRECISION)
    system = jnp.eye(size_c, dtype=jnp.float32) + delta_writing_strength[:, :, None] * strict_w * key_key
    decay_growth = jnp.exp(cumulative_decay)
    right = jnp.concatenate([delta_writing_strength[:, :, None] * value, (delta_writing_strength * decay_growth)[:, :, None] * key_vec], axis=-1)
    solved_system = lower_solve(system, right)
    state_update = solved_system[:, :, :VALUE_HEAD_SIZE] - jnp.einsum('dmj,djz->dmz', solved_system[:, :, VALUE_HEAD_SIZE:], running_state, precision=HIGH_PRECISION)
    attend = incl_w * jnp.einsum('htd,hsd->hts', query_vector, key_vec, precision=HIGH_PRECISION)
    state_readout = decay_growth[:, :, None] * jnp.einsum('cwn,cnj->cwj', query_vector, running_state, precision=HIGH_PRECISION)
    state_readout = state_readout + jnp.einsum('hts,hsv->htv', attend, state_update, precision=HIGH_PRECISION)
    trailing_keys = jnp.exp(cumulative_decay[:, -1:] - cumulative_decay)[:, :, None] * key_vec
    running_state = jnp.exp(cumulative_decay[:, -1])[:, None, None] * running_state + jnp.einsum('lpj,lpm->ljm', trailing_keys, state_update, precision=HIGH_PRECISION)
    return (running_state, state_readout)

def reference(hidden, w_query, w_key, payload_projection_matrix, conv_weight, log_decay, beta_rate, norm_gain, head_order, block_starts):
    total = hidden.shape[0]
    attention_lane_sites = jnp.arange(total).astype(jnp.int32)
    starts_tok = block_starts[attention_lane_sites // TOK_DEV]
    first = attention_lane_sites % TOK_DEV
    groups = total // GROUP
    group_first = jnp.arange(groups).astype(jnp.int32) * GROUP
    group_flag = block_starts[group_first // TOK_DEV]
    keeps = jnp.where((group_first % TOK_DEV == 0) & (group_flag == 1), 0.0, 1.0).astype(jnp.float32)

    def one_head(serve):
        logical = head_order[serve]
        key_cols = (logical * DK + jnp.arange(DK)).astype(jnp.int32)
        value_cols = (logical * 2 * VALUE_HEAD_SIZE + jnp.arange(2 * VALUE_HEAD_SIZE)).astype(jnp.int32)
        weights = jnp.concatenate([jnp.take(w_query, key_cols, axis=1), jnp.take(w_key, key_cols, axis=1), jnp.take(payload_projection_matrix, value_cols, axis=1)], axis=1)
        taps = jnp.concatenate([jnp.take(conv_weight, key_cols, axis=1), jnp.take(conv_weight, HK * DK + key_cols, axis=1), jnp.take(conv_weight, 2 * HK * DK + value_cols, axis=1)], axis=1)
        proj = jnp.dot(hidden.astype(jnp.float32), weights.astype(jnp.float32), preferred_element_type=jnp.float32).astype(jnp.bfloat16)
        mixed_in = taps[KCONV - 1].astype(jnp.float32) * proj.astype(jnp.float32)
        for lag in range(1, KCONV):
            moved = jnp.concatenate([jnp.zeros((lag, proj.shape[1]), jnp.bfloat16), proj[:-lag]], axis=0)
            blocked = (first < lag) & (starts_tok == 1)
            moved = jnp.where(blocked[:, None], jnp.zeros_like(moved), moved)
            mixed_in = mixed_in + taps[KCONV - 1 - lag].astype(jnp.float32) * moved.astype(jnp.float32)
        active = jax.nn.silu(mixed_in)
        query_vector = unit_rows(active[:, :DK])
        key_vec = unit_rows(active[:, DK:2 * DK])
        value = active[:, 2 * DK:].reshape(total, 2, VALUE_HEAD_SIZE).transpose(1, 0, 2)
        query_vector = jnp.broadcast_to(query_vector[None], (2, total, DK))
        key_vec = jnp.broadcast_to(key_vec[None], (2, total, DK))
        decay = lax.dynamic_slice_in_dim(log_decay, 2 * serve, 2, axis=0)
        delta_writing_strength = lax.dynamic_slice_in_dim(beta_rate, 2 * serve, 2, axis=0)

        def blocks(values):
            return values.reshape(2, groups, GROUP, values.shape[-1]).transpose(1, 0, 2, 3)
        inputs = (blocks(query_vector), blocks(key_vec), blocks(value), decay.reshape(2, groups, GROUP).transpose(1, 0, 2), delta_writing_strength.reshape(2, groups, GROUP).transpose(1, 0, 2), keeps)
        start = jnp.zeros((2, DK, VALUE_HEAD_SIZE), jnp.float32)
        final, reads = lax.scan(group_step, start, inputs)
        reads = reads.transpose(0, 2, 1, 3).reshape(total, 2, VALUE_HEAD_SIZE)
        scaled = reads * lax.rsqrt(lax.optimization_barrier(jnp.mean(reads * reads, axis=-1, keepdims=True)) + eps) * norm_gain
        return scaled.reshape(total, 2 * VALUE_HEAD_SIZE).astype(jnp.bfloat16)
    outputs = lax.map(one_head, jnp.arange(HK).astype(jnp.int32))
    return outputs.transpose(1, 0, 2).reshape(total, VH * VALUE_HEAD_SIZE)
```

```python
import functools

import jax
import jax.numpy as jnp
from jax import lax
from jax.experimental import pallas as pl
from jax.experimental.pallas import tpu as pltpu
from jax.sharding import PartitionSpec as P

DK = 128
VALUE_HEAD_SIZE = 128
KCONV = 4
GROUP = 64


HIGH_PRECISION = lax.Precision.HIGHEST
eps = 1e-06


def from_behind(value, axis, steps):
    count = lax.axis_size(axis)
    initial, last = (max(0, -steps), min(count, count - steps))
    return lax.ppermute(value, axis, [(source, source + steps) for source in range(initial, last)])


MESH = pl.DeviceIdType.MESH
CHUNKS = 4


def mm(a, b):
    return jnp.dot(a, b, precision=HIGH_PRECISION, preferred_element_type=jnp.float32)


def joined(later, earlier):
    both = mm(later[:, :DK], earlier)
    return jnp.concatenate([both[:, :DK], both[:, DK:] + later[:, DK:]], axis=1)


def scan_kernel(n, ab_ref, out_ref, blocks, chips, total, ring, acc, back, far, states, got, sends, recvs, ring_send, ring_recv):
    me, head = lax.axis_index("ctx"), lax.axis_index("head")
    chip, core = me // 2, lax.rem(me, 2)
    side = lax.rem(chip, 2)
    pair = chip // 2
    n_chips = n // 2
    pairs = n_chips // 2
    steps = pairs // 2
    rows = DK // CHUNKS

    def at(z, c):
        return (z * 2 + c, head)

    mate = at(chip, 1 - core)
    other = at(chip + 1 - 2 * side, core)
    ahead = at(lax.rem(chip + 2, n_chips), core)
    behind = at(lax.rem(chip + n_chips - 2, n_chips), core)
    onward = at(lax.rem(chip + n_chips + 2 - 4 * side, n_chips), core)

    barrier = pltpu.get_barrier_semaphore()
    for device in (mate, other, ahead, behind):
        pl.semaphore_signal(barrier, inc=1, device_id=device, device_id_type=MESH)
    pl.semaphore_wait(barrier, 4)

    def send(k, source, target, device):
        copy = pltpu.make_async_remote_copy(
            src_ref=source, dst_ref=target, send_sem=sends.at[k], recv_sem=recvs.at[k], device_id=device, device_id_type=MESH
        )
        copy.start()
        return copy

    first = send(0, ab_ref.at[1 - core], blocks.at[core], mate)
    blocks[core] = ab_ref[core]
    first.wait_recv()
    chips[side] = joined(blocks[1], blocks[0])
    second = send(1, chips.at[side], chips.at[side], other)
    rows_at = lax.broadcasted_iota(jnp.int32, (DK, 2 * DK), 0)
    cols_at = lax.broadcasted_iota(jnp.int32, (DK, 2 * DK), 1)
    acc[...] = jnp.where(rows_at == cols_at, 1.0, 0.0).astype(jnp.float32)
    back[...] = jnp.zeros_like(back)
    second.wait_recv()
    total[...] = joined(chips[1], chips[0])

    def hop(step, part):
        span = pl.ds(part * rows, rows)
        return pltpu.make_async_remote_copy(
            src_ref=total.at[span] if step == 0 else ring.at[step - 1, span],
            dst_ref=ring.at[step, span],
            send_sem=ring_send.at[step, part],
            recv_sem=ring_recv.at[step, part],
            device_id=onward,
            device_id_type=MESH,
        )

    for part in range(CHUNKS):
        hop(0, part).start()
    for step in range(steps):
        for part in range(CHUNKS):
            hop(step, part).wait_recv()
            if step < steps - 1:
                hop(step + 1, part).start()

        @pl.when((side == 0) & (pair >= step + 1))
        def _():
            acc[...] = joined(acc[...], ring[step])

        if step < pairs - steps - 1:

            @pl.when((side == 1) & (pair + step + 1 >= pairs))
            def _():
                back[...] = mm(ring[step, :, :DK], back[...]) + ring[step, :, DK:]

    third = send(2, acc, far, other)
    fourth = send(3, back, states.at[0], other)
    third.wait_recv()
    fourth.wait_recv()

    @pl.when(side == 0)
    def _():
        got[...] = mm(acc[:, :DK], states[0]) + acc[:, DK:]

    @pl.when(side == 1)
    def _():
        entering = mm(far[:, :DK], back[...]) + far[:, DK:]
        got[...] = mm(chips[0, :, :DK], entering) + chips[0, :, DK:]

    states[1] = got[...]
    states[2] = mm(blocks[0, :, :DK], got[...]) + blocks[0, :, DK:]
    fifth = send(4, states.at[2 - core], states.at[3], mate)
    out_ref[core] = states[1 + core]
    fifth.wait_recv()
    out_ref[1 - core] = states[3]
    for copy in (first, second, third, fourth, fifth):
        copy.wait_send()
    for step in range(steps):
        for part in range(CHUNKS):
            hop(step, part).wait_send()


def carried_in(ab, n):
    steps = n // 8
    f32 = jnp.float32
    return pl.pallas_call(
        functools.partial(scan_kernel, n),
        out_shape=jax.ShapeDtypeStruct((2, DK, DK), f32),
        in_specs=[pl.BlockSpec(memory_space=pltpu.VMEM)],
        out_specs=pl.BlockSpec(memory_space=pltpu.VMEM),
        scratch_shapes=[
            pltpu.VMEM((2, DK, 2 * DK), f32),
            pltpu.VMEM((2, DK, 2 * DK), f32),
            pltpu.VMEM((DK, 2 * DK), f32),
            pltpu.VMEM((steps, DK, 2 * DK), f32),
            pltpu.VMEM((DK, 2 * DK), f32),
            pltpu.VMEM((DK, DK), f32),
            pltpu.VMEM((DK, 2 * DK), f32),
            pltpu.VMEM((4, DK, DK), f32),
            pltpu.VMEM((DK, DK), f32),
            pltpu.SemaphoreType.DMA((5,)),
            pltpu.SemaphoreType.DMA((5,)),
            pltpu.SemaphoreType.DMA((steps, CHUNKS)),
            pltpu.SemaphoreType.DMA((steps, CHUNKS)),
        ],
        compiler_params=pltpu.CompilerParams(collective_id=0, has_side_effects=True, vmem_limit_bytes=32 << 20),
    )(ab)


def lower_solve(system, right):
    return lax.linalg.triangular_solve(
        system, right, left_side=True, lower=True, unit_diagonal=True
    )


def arrange(weight, width, head_order):
    rows = weight.shape[0]
    blocks = weight.reshape(rows, weight.shape[1] // width, width)
    return jnp.take(blocks, head_order, axis=1).reshape(rows, weight.shape[1])


def convolve(extended, weight, taps):
    proj = jnp.dot(extended, weight, preferred_element_type=jnp.float32).astype(jnp.bfloat16)
    count = proj.shape[0] - (KCONV - 1)
    total = taps[KCONV - 1].astype(jnp.float32) * proj[KCONV - 1 :].astype(jnp.float32)
    for lag in range(1, KCONV):
        offset = KCONV - 1 - lag
        total = total + taps[offset].astype(jnp.float32) * proj[offset : offset + count].astype(
            jnp.float32
        )
    return jax.nn.silu(total)


def unit_rows(values):
    return values * lax.rsqrt(jnp.sum(values * values, axis=-1, keepdims=True) + eps)


def to_blocks(values):
    count, heads, width = values.shape
    return values.reshape(count // GROUP, GROUP, heads, width).transpose(0, 2, 1, 3)


def key_phase(key_vec, decay, delta_writing_strength):
    size_c = decay.shape[-1]
    cumulative_decay = jnp.cumsum(decay, axis=-1)
    rows = lax.broadcasted_iota(jnp.int32, (size_c, size_c), 0)
    cols = lax.broadcasted_iota(jnp.int32, (size_c, size_c), 1)
    spread = cumulative_decay[..., :, None] - cumulative_decay[..., None, :]
    strict_w = jnp.where(cols < rows, jnp.exp(jnp.where(cols < rows, spread, 0.0)), 0.0)
    incl_w = jnp.where(cols <= rows, jnp.exp(jnp.where(cols <= rows, spread, 0.0)), 0.0)
    key_key = jnp.einsum("nhtd,nhsd->nhts", key_vec, key_vec, precision=HIGH_PRECISION)
    system = (
        jnp.eye(size_c, dtype=jnp.float32)
        + delta_writing_strength[..., :, None] * strict_w * key_key
    )
    decay_growth = jnp.exp(cumulative_decay)
    write_k = lower_solve(system, (delta_writing_strength * decay_growth)[..., None] * key_vec)
    trailing_keys = jnp.exp(cumulative_decay[..., -1:] - cumulative_decay)[..., None] * key_vec
    eye_k = jnp.eye(DK, dtype=jnp.float32)
    trans_a = jnp.exp(cumulative_decay[..., -1])[..., None, None] * eye_k - jnp.einsum(
        "nhsk,nhsj->nhkj", trailing_keys, write_k, precision=HIGH_PRECISION
    )

    def key_chain(acc, step_a):
        return (jnp.einsum("hij,hjk->hik", step_a, acc, precision=HIGH_PRECISION), acc)

    start = jnp.broadcast_to(eye_k, (key_vec.shape[1], DK, DK))
    dev_a, enter_a = lax.scan(key_chain, start, trans_a)
    return (key_vec, decay_growth, incl_w, system, write_k, trailing_keys, trans_a, enter_a, dev_a)


def value_phase(query_vector, value, delta_writing_strength, keyed):
    key_vec, decay_growth, incl_w, system, write_k, trailing_keys, trans_a, enter_a, dev_a = keyed
    write_v = lower_solve(system, delta_writing_strength[..., None] * value)
    attend = incl_w * jnp.einsum("nhtd,nhsd->nhts", query_vector, key_vec, precision=HIGH_PRECISION)
    inner = jnp.einsum("nhts,nhsv->nhtv", attend, write_v, precision=HIGH_PRECISION)
    qeff = decay_growth[..., None] * query_vector - jnp.einsum(
        "nhts,nhsk->nhtk", attend, write_k, precision=HIGH_PRECISION
    )
    trans_b = jnp.einsum("nhsk,nhsv->nhkv", trailing_keys, write_v, precision=HIGH_PRECISION)

    def value_chain(acc, pair):
        return (jnp.einsum("hij,hjv->hiv", pair[0], acc, precision=HIGH_PRECISION) + pair[1], acc)

    start = jnp.zeros((value.shape[1], DK, VALUE_HEAD_SIZE), jnp.float32)
    dev_b, enter_b = lax.scan(value_chain, start, (trans_a, trans_b))
    return (inner, qeff, enter_b, dev_b)


def per_device(
    hidden,
    w_query,
    w_key,
    payload_projection_matrix,
    conv_weight,
    log_decay,
    beta_rate,
    norm_gain,
    head_order,
    block_starts,
):
    count = hidden.shape[0]
    key_heads = head_order.shape[0] // lax.axis_size("head")
    heads = 2 * key_heads
    serve = lax.axis_index("head")
    mine = lax.dynamic_slice_in_dim(head_order, serve * key_heads, key_heads)
    key_cols = (mine[:, None] * DK + jnp.arange(DK, dtype=jnp.int32)[None, :]).reshape(-1)
    value_cols = (
        mine[:, None] * (2 * VALUE_HEAD_SIZE)
        + jnp.arange(2 * VALUE_HEAD_SIZE, dtype=jnp.int32)[None, :]
    ).reshape(-1)
    key_total = head_order.shape[0] * DK
    question_filter_weights = jnp.take(conv_weight, key_cols, axis=1)
    taps_k = jnp.take(conv_weight, key_total + key_cols, axis=1)
    taps_v = jnp.take(conv_weight, 2 * key_total + value_cols, axis=1)
    keep = (1 - block_starts[0]).astype(jnp.float32)
    rim = from_behind(hidden[count - (KCONV - 1) :], "ctx", 1)
    extended = jnp.concatenate([rim * keep.astype(jnp.bfloat16), hidden], axis=0)
    decay = log_decay.reshape(heads, count // GROUP, GROUP).transpose(1, 0, 2)
    delta_writing_strength = beta_rate.reshape(heads, count // GROUP, GROUP).transpose(1, 0, 2)
    cols_q, cols_k, cols_v = (
        lax.all_to_all(
            arrange(w_query, DK, head_order), "head", split_axis=1, concat_axis=0, tiled=True
        ),
        lax.all_to_all(
            arrange(w_key, DK, head_order), "head", split_axis=1, concat_axis=0, tiled=True
        ),
        lax.all_to_all(
            arrange(payload_projection_matrix, 2 * VALUE_HEAD_SIZE, head_order),
            "head",
            split_axis=1,
            concat_axis=0,
            tiled=True,
        ),
    )
    key_act = convolve(extended, cols_k, taps_k)
    key_vec = to_blocks(jnp.repeat(unit_rows(key_act.reshape(count, key_heads, DK)), 2, axis=1))
    keyed = key_phase(key_vec, decay, delta_writing_strength)
    query_act = convolve(extended, cols_q, question_filter_weights)
    value_act = convolve(extended, cols_v, taps_v)
    query_vector = to_blocks(
        jnp.repeat(unit_rows(query_act.reshape(count, key_heads, DK)), 2, axis=1)
    )
    value = to_blocks(value_act.reshape(count, heads, VALUE_HEAD_SIZE))
    inner, qeff, enter_b, dev_b = value_phase(query_vector, value, delta_writing_strength, keyed)
    enter_a = keyed[7]
    dev_a = keyed[8]
    prior_b = carried_in(jnp.concatenate([dev_a * keep, dev_b], axis=-1), lax.axis_size("ctx"))
    state_in = prior_b * keep
    entering = jnp.einsum("nhij,hjv->nhiv", enter_a, state_in, precision=HIGH_PRECISION) + enter_b
    reads = inner + jnp.einsum("nhtk,nhkv->nhtv", qeff, entering, precision=HIGH_PRECISION)
    reads = reads.transpose(0, 2, 1, 3).reshape(count, heads, VALUE_HEAD_SIZE)
    scaled = reads * lax.rsqrt(jnp.mean(reads * reads, axis=-1, keepdims=True) + eps) * norm_gain
    return scaled.reshape(count, heads * VALUE_HEAD_SIZE).astype(jnp.bfloat16)


def solution(mesh):
    return jax.shard_map(
        per_device,
        mesh=mesh,
        in_specs=(
            P("ctx", None),
            P("head", None),
            P("head", None),
            P("head", None),
            P(),
            P("head", "ctx"),
            P("head", "ctx"),
            P(),
            P(),
            P("ctx"),
        ),
        out_specs=P("ctx", "head"),
        check_vma=False,
    )
```

```python
import functools

import jax
import jax.numpy as jnp
from jax import lax
from jax.experimental import pallas as pl
from jax.experimental.pallas import tpu as pltpu
from jax.sharding import PartitionSpec as P

DK = 128
VALUE_HEAD_SIZE = 128
KCONV = 4
GROUP = 64
RIM = 16
SIDE = 4
CHUNKS = 4

MESH = pl.DeviceIdType.MESH
HIGH_PRECISION = lax.Precision.HIGHEST
F32 = jnp.float32
BF16 = jnp.bfloat16
eps = 1e-06


def split(a):
    high = a.astype(BF16)
    return high, (a - high.astype(F32)).astype(BF16)


def mm(a, b, left=1, right=0):
    def dot(x, y):
        return lax.dot_general(x, y, (((left,), (right,)), ((), ())), preferred_element_type=F32)

    return dot(a[0], b[0]) + (dot(a[0], b[1]) + dot(a[1], b[0]))


def exact(a, b, left=1, right=0):
    return lax.dot_general(
        a, b, (((left,), (right,)), ((), ())), precision=HIGH_PRECISION, preferred_element_type=F32
    )


def exchange_kernel(
    order_ref, query_ref, key_ref, value_ref, hidden_ref, w_ref, ext_ref,
    query, key, value, stage, load_sem, send_sem, recv_sem, pass_send, pass_recv, rim_sem, local_sem,
):
    me, head = lax.axis_index("ctx"), lax.axis_index("head")
    n, heads = lax.axis_size("ctx"), lax.axis_size("head")
    chip, core = me // 2, lax.rem(me, 2)
    x, y = head // SIDE, lax.rem(head, SIDE)
    shard = query_ref.shape[0]
    half = shard // 2
    count = hidden_ref.shape[0]
    mine = pl.ds(pl.multiple_of(core * half, half), half)
    loads = []
    for j in range(heads):
        narrow, wide = pl.ds(j * DK, DK), pl.ds(2 * j * DK, 2 * DK)
        for i, (source, columns, target) in enumerate(
            ((query_ref, narrow, query), (key_ref, narrow, key), (value_ref, wide, value))
        ):
            loads.append(pltpu.make_async_copy(source.at[mine, columns], target.at[j], load_sem.at[i, j]))
    for load in loads:
        load.start()
    body = pltpu.make_async_copy(hidden_ref, ext_ref.at[pl.ds(RIM, count)], local_sem.at[0])
    body.start()

    def peer(dx, dy):
        return lax.rem(x + dx, SIDE) * SIDE + lax.rem(y + dy, SIDE)

    offsets = sorted(
        ((dx, dy) for dx in range(SIDE) for dy in range(SIDE)),
        key=lambda o: (-(min(o[0], SIDE - o[0]) + min(o[1], SIDE - o[1])), o),
    )[: heads - 1]
    mate = (chip * 2 + 1 - core, head)
    following = (lax.rem(me + 1, n), head)
    previous = (lax.rem(me + n - 1, n), head)
    barrier = pltpu.get_barrier_semaphore()
    for device in [(me, peer(dx, dy)) for dx, dy in offsets] + [mate, following, previous]:
        pl.semaphore_signal(barrier, inc=1, device_id=device, device_id_type=MESH)
    for load in loads:
        load.wait()
    pl.semaphore_wait(barrier, heads + 2)

    rim = pltpu.make_async_remote_copy(
        src_ref=hidden_ref.at[pl.ds(count - RIM, RIM)],
        dst_ref=ext_ref.at[pl.ds(0, RIM)],
        send_sem=rim_sem.at[0],
        recv_sem=rim_sem.at[1],
        device_id=following,
        device_id_type=MESH,
    )
    rim.start()

    def rows_of(source):
        return pl.ds(pl.multiple_of(source * shard + core * half, half), half)

    def prepare(k, serve):
        logical = order_ref[serve]
        stage[k, :, :DK] = query[logical]
        stage[k, :, DK : 2 * DK] = key[logical]
        stage[k, :, 2 * DK :] = value[logical]

    sent = []
    for k, (dx, dy) in enumerate(offsets):
        target = peer(dx, dy)
        prepare(k, target)
        copy = pltpu.make_async_remote_copy(
            src_ref=stage.at[k],
            dst_ref=w_ref.at[rows_of(head)],
            send_sem=send_sem.at[k],
            recv_sem=recv_sem.at[k],
            device_id=(me, target),
            device_id_type=MESH,
        )
        copy.start()
        sent.append(copy)
    last = heads - 1
    prepare(last, head)
    own = pltpu.make_async_copy(stage.at[last], w_ref.at[rows_of(head)], local_sem.at[1])
    own.start()

    def passing(k, source, source_ref):
        return pltpu.make_async_remote_copy(
            src_ref=source_ref,
            dst_ref=w_ref.at[rows_of(source)],
            send_sem=pass_send.at[k],
            recv_sem=pass_recv.at[k],
            device_id=mate,
            device_id_type=MESH,
        )

    passed = [passing(last, head, stage.at[last])]
    passed[0].start()
    for k in reversed(range(last)):
        dx, dy = offsets[k]
        source = peer(SIDE - dx, SIDE - dy)
        sent[k].wait_recv()
        copy = passing(k, source, w_ref.at[rows_of(source)])
        copy.start()
        passed.append(copy)
    body.wait()
    own.wait()
    for copy in sent:
        copy.wait_send()
    for copy in passed:
        copy.wait()
    rim.wait()


def exchange(head_order, w_query, w_key, w_value, hidden):
    heads, shard = head_order.shape[0], w_query.shape[0]
    half, width = shard // 2, 4 * DK
    whole = pl.BlockSpec(memory_space=pl.ANY)
    dma = pltpu.SemaphoreType.DMA
    return pl.pallas_call(
        exchange_kernel,
        out_shape=(
            jax.ShapeDtypeStruct((heads * shard, width), BF16),
            jax.ShapeDtypeStruct((hidden.shape[0] + RIM, hidden.shape[1]), BF16),
        ),
        in_specs=[pl.BlockSpec(memory_space=pltpu.SMEM)] + [whole] * 4,
        out_specs=(whole, whole),
        scratch_shapes=[
            pltpu.VMEM((heads, half, DK), BF16),
            pltpu.VMEM((heads, half, DK), BF16),
            pltpu.VMEM((heads, half, 2 * DK), BF16),
            pltpu.VMEM((heads, half, width), BF16),
            dma((3, heads)), dma((heads,)), dma((heads,)), dma((heads,)), dma((heads,)), dma((2,)), dma((2,)),
        ],
        compiler_params=pltpu.CompilerParams(collective_id=1, has_side_effects=True),
    )(head_order, w_query, w_key, w_value, hidden)


def local_kernel(
    order_ref, starts_ref, ext_ref, w_ref, conv_ref, decay_ref, beta_ref, ab_ref, reach_ref, inner_ref, proj
):
    count = ext_ref.shape[0] - RIM
    groups = count // GROUP
    key_total = order_ref.shape[0] * DK
    logical = order_ref[lax.axis_index("head")]
    keep = jnp.where(starts_ref[0] == 0, 1.0, 0.0).astype(F32)
    edge = jnp.where(lax.axis_index("ctx") > 0, keep, 0.0)
    raw = jnp.dot(ext_ref[...], w_ref[...], preferred_element_type=F32).astype(BF16).astype(F32)
    proj[RIM:] = raw[RIM:]
    proj[:RIM] = raw[:RIM] * edge

    def act(column, width, start):
        taps = conv_ref[:, pl.ds(pl.multiple_of(start, DK), width)].astype(F32)
        columns = slice(column, column + width)
        total = taps[KCONV - 1 : KCONV] * proj[RIM:, columns]
        for lag in range(1, KCONV):
            at = KCONV - 1 - lag
            total = total + taps[at : at + 1] * proj[RIM - lag : RIM - lag + count, columns]
        return total / (1.0 + jnp.exp(-total))

    def unit(values):
        return values * lax.rsqrt(jnp.sum(values * values, axis=-1, keepdims=True) + eps)

    key = unit(act(DK, DK, key_total + logical * DK))
    query = unit(act(0, DK, logical * DK))
    values = [act((2 + h) * DK, DK, 2 * key_total + (2 * logical + h) * DK) for h in range(2)]

    decay, beta = decay_ref[...], beta_ref[...]
    row = lax.broadcasted_iota(jnp.int32, (count, count), 0)
    col = lax.broadcasted_iota(jnp.int32, (count, count), 1)
    within = ((col <= row) & (col // GROUP == row // GROUP)).astype(F32)
    sums = exact(within, decay, 1, 1)
    strength = exact((row == col).astype(F32), beta, 1, 1)
    token = lax.broadcasted_iota(jnp.int32, (count, GROUP), 0)
    place = lax.broadcasted_iota(jnp.int32, (count, GROUP), 1)

    r = lax.broadcasted_iota(jnp.int32, (GROUP, GROUP), 0)
    c = lax.broadcasted_iota(jnp.int32, (GROUP, GROUP), 1)
    eye = (r == c).astype(F32)
    eye_k = (
        lax.broadcasted_iota(jnp.int32, (DK, DK), 0) == lax.broadcasted_iota(jnp.int32, (DK, DK), 1)
    ).astype(F32)

    def below(size):
        return (r // (2 * size) == c // (2 * size)) & (r // size != c // size) & (c < r)

    tasks = []
    for g in range(groups):
        span = slice(g * GROUP, (g + 1) * GROUP)
        along = exact(decay, ((token // GROUP == g) & (token - g * GROUP <= place)).astype(F32))
        k_g, q_g = key[span], query[span]
        k_s, q_s = split(k_g), split(q_g)
        key_key, query_key = mm(k_s, k_s, 1, 1), mm(q_s, k_s, 1, 1)
        for h in range(2):
            down = sums[span, h : h + 1]
            b = strength[span, h : h + 1]
            spread = jnp.exp(jnp.where(c <= r, down - along[h : h + 1], 0.0))
            system = jnp.where(c < r, b * spread * key_key, 0.0)
            attend = jnp.where(c <= r, spread * query_key, 0.0)
            grown = jnp.exp(down)
            end = down[GROUP - 1 : GROUP]
            tasks.append(
                dict(
                    h=h, g=g, system=system, attend=split(attend), q=grown * q_g, end=jnp.exp(end),
                    right=split(jnp.concatenate([b * values[h][span], (b * grown) * k_g], axis=1)),
                    trailing=split(jnp.exp(end - down) * k_g),
                    inverse=eye - jnp.where(below(1), system, 0.0),
                )
            )
    size = 2
    while size < GROUP:
        mask = below(size)
        for t in tasks:
            t["split"] = split(t["inverse"])
            t["half"] = mm(split(jnp.where(mask, t["system"], 0.0)), t["split"])
        for t in tasks:
            t["inverse"] = t["inverse"] - mm(t["split"], split(t["half"]))
        size *= 2
    for t in tasks:
        t["writes"] = split(mm(split(t["inverse"]), t["right"]))
    for t in tasks:
        seen = mm(t["attend"], t["writes"])
        t["inner"] = seen[:, :DK]
        t["reach"] = t["q"] - seen[:, DK:]
        moved = mm(t["trailing"], t["writes"], 0, 0)
        t["a"] = t["end"] * eye_k - moved[:, DK:]
        t["b"] = moved[:, :DK]
    whole = [None, None]
    for t in tasks:
        h, span = t["h"], slice(t["g"] * GROUP, (t["g"] + 1) * GROUP)
        if t["g"] == 0:
            reach_ref[h, span] = t["reach"] * keep
            inner_ref[h, span] = t["inner"]
            whole[h] = jnp.concatenate([t["a"], t["b"]], axis=1)
        else:
            entering = split(whole[h])
            both = mm(split(t["reach"]), entering)
            reach_ref[h, span] = both[:, :DK] * keep
            inner_ref[h, span] = t["inner"] + both[:, DK:]
            step = mm(split(t["a"]), entering)
            whole[h] = jnp.concatenate([step[:, :DK], step[:, DK:] + t["b"]], axis=1)
    for h in range(2):
        ab_ref[h, :, :DK] = whole[h][:, :DK] * keep
        ab_ref[h, :, DK:] = whole[h][:, DK:]


def local(head_order, block_starts, ext, w, conv_weight, log_decay, beta_rate):
    count = ext.shape[0] - RIM
    smem, vmem = pl.BlockSpec(memory_space=pltpu.SMEM), pl.BlockSpec(memory_space=pltpu.VMEM)
    return pl.pallas_call(
        local_kernel,
        out_shape=(
            jax.ShapeDtypeStruct((2, DK, 2 * DK), F32),
            jax.ShapeDtypeStruct((2, count, DK), F32),
            jax.ShapeDtypeStruct((2, count, DK), F32),
        ),
        in_specs=[smem, smem] + [vmem] * 5,
        out_specs=(vmem, vmem, vmem),
        scratch_shapes=[pltpu.VMEM((count + RIM, 4 * DK), F32)],
        compiler_params=pltpu.CompilerParams(vmem_limit_bytes=48 << 20),
    )(head_order, block_starts, ext, w, conv_weight, log_decay, beta_rate)


def joined(later, earlier):
    both = mm(split(later[:, :DK]), split(earlier))
    return jnp.concatenate([both[:, :DK], both[:, DK:] + later[:, DK:]], axis=1)


def scan_kernel(
    n, ab_ref, reach_ref, inner_ref, gain_ref, out_ref, blocks, chips, total, ring, acc, back, far, states, got, sends, recvs, ring_send, ring_recv
):
    me, head = lax.axis_index("ctx"), lax.axis_index("head")
    chip, core = me // 2, lax.rem(me, 2)
    side = lax.rem(chip, 2)
    pair = chip // 2
    n_chips = n // 2
    pairs = n_chips // 2
    steps = pairs // 2
    rows = DK // CHUNKS

    def at(z, c):
        return (z * 2 + c, head)

    mate = at(chip, 1 - core)
    other = at(chip + 1 - 2 * side, core)
    ahead = at(lax.rem(chip + 2, n_chips), core)
    behind = at(lax.rem(chip + n_chips - 2, n_chips), core)
    onward = at(lax.rem(chip + n_chips + 2 - 4 * side, n_chips), core)

    barrier = pltpu.get_barrier_semaphore()
    for device in (mate, other, ahead, behind):
        pl.semaphore_signal(barrier, inc=1, device_id=device, device_id_type=MESH)
    pl.semaphore_wait(barrier, 4)

    def send(k, source, target, device):
        copy = pltpu.make_async_remote_copy(
            src_ref=source, dst_ref=target, send_sem=sends.at[k], recv_sem=recvs.at[k], device_id=device, device_id_type=MESH
        )
        copy.start()
        return copy

    first = send(0, ab_ref.at[1 - core], blocks.at[core], mate)
    blocks[core] = ab_ref[core]
    first.wait_recv()
    chips[side] = joined(blocks[1], blocks[0])
    second = send(1, chips.at[side], chips.at[side], other)
    rows_at = lax.broadcasted_iota(jnp.int32, (DK, 2 * DK), 0)
    cols_at = lax.broadcasted_iota(jnp.int32, (DK, 2 * DK), 1)
    acc[...] = jnp.where(rows_at == cols_at, 1.0, 0.0).astype(jnp.float32)
    back[...] = jnp.zeros_like(back)
    second.wait_recv()
    total[...] = joined(chips[1], chips[0])

    def hop(step, part):
        span = pl.ds(part * rows, rows)
        return pltpu.make_async_remote_copy(
            src_ref=total.at[span] if step == 0 else ring.at[step - 1, span],
            dst_ref=ring.at[step, span],
            send_sem=ring_send.at[step, part],
            recv_sem=ring_recv.at[step, part],
            device_id=onward,
            device_id_type=MESH,
        )

    for part in range(CHUNKS):
        hop(0, part).start()
    for step in range(steps):
        for part in range(CHUNKS):
            hop(step, part).wait_recv()
            if step < steps - 1:
                hop(step + 1, part).start()

        @pl.when((side == 0) & (pair >= step + 1))
        def _():
            acc[...] = joined(acc[...], ring[step])

        if step < pairs - steps - 1:

            @pl.when((side == 1) & (pair + step + 1 >= pairs))
            def _():
                back[...] = mm(split(ring[step, :, :DK]), split(back[...])) + ring[step, :, DK:]

    third = send(2, acc, far, other)
    fourth = send(3, back, states.at[0], other)
    third.wait_recv()
    fourth.wait_recv()

    @pl.when(side == 0)
    def _():
        got[...] = mm(split(acc[:, :DK]), split(states[0])) + acc[:, DK:]

    @pl.when(side == 1)
    def _():
        entering = mm(split(far[:, :DK]), split(back[...])) + far[:, DK:]
        got[...] = mm(split(chips[0, :, :DK]), split(entering)) + chips[0, :, DK:]

    states[1] = got[...]
    states[2] = mm(split(blocks[0, :, :DK]), split(got[...])) + blocks[0, :, DK:]
    fifth = send(4, states.at[2 - core], states.at[3], mate)

    def read(h, state):
        reads = inner_ref[h] + mm(split(reach_ref[h]), split(state))
        scaled = reads * lax.rsqrt(jnp.mean(reads * reads, axis=-1, keepdims=True) + eps) * gain_ref[...]
        out_ref[:, pl.ds(pl.multiple_of(h * DK, DK), DK)] = scaled.astype(BF16)

    read(core, states[1 + core])
    fifth.wait_recv()
    read(1 - core, states[3])
    for copy in (first, second, third, fourth, fifth):
        copy.wait_send()
    for step in range(steps):
        for part in range(CHUNKS):
            hop(step, part).wait_send()


def read_out(ab, reach, inner, norm_gain, n):
    steps = n // 8
    count = reach.shape[1]
    vmem = pl.BlockSpec(memory_space=pltpu.VMEM)
    dma = pltpu.SemaphoreType.DMA
    pair = pltpu.VMEM((2, DK, 2 * DK), F32)
    one = pltpu.VMEM((DK, 2 * DK), F32)
    state = pltpu.VMEM((DK, DK), F32)
    return pl.pallas_call(
        functools.partial(scan_kernel, n),
        out_shape=jax.ShapeDtypeStruct((count, 2 * DK), BF16),
        in_specs=[vmem] * 4,
        out_specs=vmem,
        scratch_shapes=[
            pair, pair, one, pltpu.VMEM((steps, DK, 2 * DK), F32), one, state, one, pltpu.VMEM((4, DK, DK), F32), state,
            dma((5,)), dma((5,)), dma((steps, CHUNKS)), dma((steps, CHUNKS)),
        ],
        compiler_params=pltpu.CompilerParams(collective_id=0, has_side_effects=True, vmem_limit_bytes=32 << 20),
    )(ab, reach, inner, norm_gain.reshape(1, DK))


def per_device(
    hidden,
    w_query,
    w_key,
    payload_projection_matrix,
    conv_weight,
    log_decay,
    beta_rate,
    norm_gain,
    head_order,
    block_starts,
):
    w, ext = exchange(head_order, w_query, w_key, payload_projection_matrix, hidden)
    ab, reach, inner = local(head_order, block_starts, ext, w, conv_weight, log_decay, beta_rate)
    return read_out(ab, reach, inner, norm_gain, lax.axis_size("ctx"))


def solution(mesh):
    return jax.shard_map(
        per_device,
        mesh=mesh,
        in_specs=(
            P("ctx", None),
            P("head", None),
            P("head", None),
            P("head", None),
            P(),
            P("head", "ctx"),
            P("head", "ctx"),
            P(),
            P(),
            P("ctx"),
        ),
        out_specs=P("ctx", "head"),
        check_vma=False,
    )
```

```python
import functools

import jax
import jax.numpy as jnp
from jax import lax
from jax.experimental import pallas as pl
from jax.experimental.pallas import tpu as pltpu
from jax.sharding import PartitionSpec as P

DK = 128
VALUE_HEAD_SIZE = 128
KCONV = 4
GROUP = 64
RIM = 16
SIDE = 4
CHUNKS = 4
QUAD = 4
PARTS = 2

MESH = pl.DeviceIdType.MESH
HIGH_PRECISION = lax.Precision.HIGHEST
F32 = jnp.float32
BF16 = jnp.bfloat16
eps = 1e-06


def split(a):
    high = a.astype(BF16)
    return high, (a - high.astype(F32)).astype(BF16)


def mm(a, b, left=1, right=0):
    def dot(x, y):
        return lax.dot_general(x, y, (((left,), (right,)), ((), ())), preferred_element_type=F32)

    return dot(a[0], b[0]) + (dot(a[0], b[1]) + dot(a[1], b[0]))


def exact(a, b, left=1, right=0):
    return lax.dot_general(
        a, b, (((left,), (right,)), ((), ())), precision=HIGH_PRECISION, preferred_element_type=F32
    )


def exchange_kernel(
    order_ref, query_ref, key_ref, value_ref, hidden_ref, w_ref, rim_ref,
    query, key, value, stage, load_sem, send_sem, recv_sem, pass_send, pass_recv, rim_sem, local_sem,
):
    me, head = lax.axis_index("ctx"), lax.axis_index("head")
    n, heads = lax.axis_size("ctx"), lax.axis_size("head")
    chip, core = me // 2, lax.rem(me, 2)
    x, y = head // SIDE, lax.rem(head, SIDE)
    shard = query_ref.shape[0]
    half = shard // 2
    count = hidden_ref.shape[0]
    mine = pl.ds(pl.multiple_of(core * half, half), half)
    loads = []
    for j in range(heads):
        narrow, wide = pl.ds(j * DK, DK), pl.ds(2 * j * DK, 2 * DK)
        for i, (source, columns, target) in enumerate(
            ((query_ref, narrow, query), (key_ref, narrow, key), (value_ref, wide, value))
        ):
            loads.append(pltpu.make_async_copy(source.at[mine, columns], target.at[j], load_sem.at[i, j]))
    for load in loads:
        load.start()

    def peer(dx, dy):
        return lax.rem(x + dx, SIDE) * SIDE + lax.rem(y + dy, SIDE)

    offsets = sorted(
        ((dx, dy) for dx in range(SIDE) for dy in range(SIDE)),
        key=lambda o: (-(min(o[0], SIDE - o[0]) + min(o[1], SIDE - o[1])), o),
    )[: heads - 1]
    mate = (chip * 2 + 1 - core, head)
    following = (lax.rem(me + 1, n), head)
    previous = (lax.rem(me + n - 1, n), head)
    barrier = pltpu.get_barrier_semaphore()
    for device in [(me, peer(dx, dy)) for dx, dy in offsets] + [mate]:
        pl.semaphore_signal(barrier, inc=1, device_id=device, device_id_type=MESH)

    @pl.when(me > 0)
    def _():
        pl.semaphore_signal(barrier, inc=1, device_id=previous, device_id_type=MESH)

    def prepare(k, serve):
        logical = order_ref[serve]
        stage[k, :, :DK] = query[logical]
        stage[k, :, DK : 2 * DK] = key[logical]
        stage[k, :, 2 * DK :] = value[logical]

    for load in loads:
        load.wait()
    last = heads - 1
    for k, (dx, dy) in enumerate(offsets):
        prepare(k, peer(dx, dy))
    prepare(last, head)
    pl.semaphore_wait(barrier, heads + 1 - (me + 1) // n)


    rim = pltpu.make_async_remote_copy(
        src_ref=hidden_ref.at[pl.ds(count - RIM, RIM)],
        dst_ref=rim_ref,
        send_sem=rim_sem.at[0],
        recv_sem=rim_sem.at[1],
        device_id=following,
        device_id_type=MESH,
    )

    @pl.when(me < n - 1)
    def _():
        rim.start()

    def rows_of(source):
        return pl.ds(pl.multiple_of(source * shard + core * half, half), half)

    sent = []
    for k, (dx, dy) in enumerate(offsets):
        target = peer(dx, dy)
        copy = pltpu.make_async_remote_copy(
            src_ref=stage.at[k],
            dst_ref=w_ref.at[rows_of(head)],
            send_sem=send_sem.at[k],
            recv_sem=recv_sem.at[k],
            device_id=(me, target),
            device_id_type=MESH,
        )
        copy.start()
        sent.append(copy)
    own = pltpu.make_async_copy(stage.at[last], w_ref.at[rows_of(head)], local_sem.at[0])
    own.start()

    def passing(k, source, source_ref):
        return pltpu.make_async_remote_copy(
            src_ref=source_ref,
            dst_ref=w_ref.at[rows_of(source)],
            send_sem=pass_send.at[k],
            recv_sem=pass_recv.at[k],
            device_id=mate,
            device_id_type=MESH,
        )

    passed = [passing(last, head, stage.at[last])]
    passed[0].start()
    for k in reversed(range(last)):
        dx, dy = offsets[k]
        source = peer(SIDE - dx, SIDE - dy)
        sent[k].wait_recv()
        copy = passing(k, source, w_ref.at[rows_of(source)])
        copy.start()
        passed.append(copy)
    own.wait()
    for copy in sent:
        copy.wait_send()
    for copy in passed:
        copy.wait()

    @pl.when(me < n - 1)
    def _():
        rim.wait_send()

    @pl.when(me > 0)
    def _():
        rim.wait_recv()


def exchange(head_order, w_query, w_key, w_value, hidden):
    heads, shard = head_order.shape[0], w_query.shape[0]
    half, width = shard // 2, 4 * DK
    whole = pl.BlockSpec(memory_space=pl.ANY)
    dma = pltpu.SemaphoreType.DMA
    return pl.pallas_call(
        exchange_kernel,
        out_shape=(
            jax.ShapeDtypeStruct((heads * shard, width), BF16),
            jax.ShapeDtypeStruct((RIM, hidden.shape[1]), BF16),
        ),
        in_specs=[pl.BlockSpec(memory_space=pltpu.SMEM)] + [whole] * 4,
        out_specs=(whole, whole),
        scratch_shapes=[
            pltpu.VMEM((heads, half, DK), BF16),
            pltpu.VMEM((heads, half, DK), BF16),
            pltpu.VMEM((heads, half, 2 * DK), BF16),
            pltpu.VMEM((heads, half, width), BF16),
            dma((3, heads)), dma((heads,)), dma((heads,)), dma((heads,)), dma((heads,)), dma((2,)), dma((1,)),
        ],
        compiler_params=pltpu.CompilerParams(collective_id=1, has_side_effects=True),
    )(head_order, w_query, w_key, w_value, hidden)


def local_kernel(
    order_ref, starts_ref, rim_ref, hidden_ref, w_ref, conv_ref, decay_ref, beta_ref, ab_ref, reach_ref, inner_ref, proj
):
    count = hidden_ref.shape[0]
    groups = count // GROUP
    key_total = order_ref.shape[0] * DK
    logical = order_ref[lax.axis_index("head")]
    keep = jnp.where(starts_ref[0] == 0, 1.0, 0.0).astype(F32)
    edge = jnp.where(lax.axis_index("ctx") > 0, keep, 0.0)
    extended = jnp.concatenate([rim_ref[...], hidden_ref[...]], axis=0)
    raw = jnp.dot(extended, w_ref[...], preferred_element_type=F32).astype(BF16).astype(F32)
    proj[RIM:] = raw[RIM:]
    proj[:RIM] = jnp.where(edge > 0.0, raw[:RIM], 0.0)

    def act(column, width, start):
        taps = conv_ref[:, pl.ds(pl.multiple_of(start, DK), width)].astype(F32)
        columns = slice(column, column + width)
        total = taps[KCONV - 1 : KCONV] * proj[RIM:, columns]
        for lag in range(1, KCONV):
            at = KCONV - 1 - lag
            total = total + taps[at : at + 1] * proj[RIM - lag : RIM - lag + count, columns]
        return total / (1.0 + jnp.exp(-total))

    def unit(values):
        return values * lax.rsqrt(jnp.sum(values * values, axis=-1, keepdims=True) + eps)

    key = unit(act(DK, DK, key_total + logical * DK))
    query = unit(act(0, DK, logical * DK))
    values = [act((2 + h) * DK, DK, 2 * key_total + (2 * logical + h) * DK) for h in range(2)]

    decay, beta = decay_ref[...], beta_ref[...]
    row = lax.broadcasted_iota(jnp.int32, (count, count), 0)
    col = lax.broadcasted_iota(jnp.int32, (count, count), 1)
    within = ((col <= row) & (col // GROUP == row // GROUP)).astype(F32)
    sums = exact(within, decay, 1, 1)
    strength = exact((row == col).astype(F32), beta, 1, 1)
    token = lax.broadcasted_iota(jnp.int32, (count, GROUP), 0)
    place = lax.broadcasted_iota(jnp.int32, (count, GROUP), 1)

    r = lax.broadcasted_iota(jnp.int32, (GROUP, GROUP), 0)
    c = lax.broadcasted_iota(jnp.int32, (GROUP, GROUP), 1)
    eye = (r == c).astype(F32)
    eye_k = (
        lax.broadcasted_iota(jnp.int32, (DK, DK), 0) == lax.broadcasted_iota(jnp.int32, (DK, DK), 1)
    ).astype(F32)

    def below(size):
        return (r // (2 * size) == c // (2 * size)) & (r // size != c // size) & (c < r)

    tasks = []
    for g in range(groups):
        span = slice(g * GROUP, (g + 1) * GROUP)
        along = exact(decay, ((token // GROUP == g) & (token - g * GROUP <= place)).astype(F32))
        k_g, q_g = key[span], query[span]
        k_s, q_s = split(k_g), split(q_g)
        key_key, query_key = mm(k_s, k_s, 1, 1), mm(q_s, k_s, 1, 1)
        for h in range(2):
            down = sums[span, h : h + 1]
            b = strength[span, h : h + 1]
            spread = jnp.exp(jnp.where(c <= r, down - along[h : h + 1], 0.0))
            system = jnp.where(c < r, b * spread * key_key, 0.0)
            attend = jnp.where(c <= r, spread * query_key, 0.0)
            grown = jnp.exp(down)
            end = down[GROUP - 1 : GROUP]
            tasks.append(
                dict(
                    h=h, g=g, system=system, attend=split(attend), q=grown * q_g, end=jnp.exp(end),
                    right=split(jnp.concatenate([b * values[h][span], (b * grown) * k_g], axis=1)),
                    trailing=split(jnp.exp(end - down) * k_g),
                    inverse=eye - jnp.where(below(1), system, 0.0),
                )
            )
    size = 2
    while size < GROUP:
        mask = below(size)
        for t in tasks:
            t["split"] = split(t["inverse"])
            t["half"] = mm(split(jnp.where(mask, t["system"], 0.0)), t["split"])
        for t in tasks:
            t["inverse"] = t["inverse"] - mm(t["split"], split(t["half"]))
        size *= 2
    for t in tasks:
        t["writes"] = split(mm(split(t["inverse"]), t["right"]))
    for t in tasks:
        seen = mm(t["attend"], t["writes"])
        t["inner"] = seen[:, :DK]
        t["reach"] = t["q"] - seen[:, DK:]
        moved = mm(t["trailing"], t["writes"], 0, 0)
        t["a"] = t["end"] * eye_k - moved[:, DK:]
        t["b"] = moved[:, :DK]
    whole = [None, None]
    for t in tasks:
        h, span = t["h"], slice(t["g"] * GROUP, (t["g"] + 1) * GROUP)
        if t["g"] == 0:
            reach_ref[h, span] = t["reach"] * keep
            inner_ref[h, span] = t["inner"]
            whole[h] = jnp.concatenate([t["a"], t["b"]], axis=1)
        else:
            entering = split(whole[h])
            both = mm(split(t["reach"]), entering)
            reach_ref[h, span] = both[:, :DK] * keep
            inner_ref[h, span] = t["inner"] + both[:, DK:]
            step = mm(split(t["a"]), entering)
            whole[h] = jnp.concatenate([step[:, :DK], step[:, DK:] + t["b"]], axis=1)
    for h in range(2):
        ab_ref[h, :, :DK] = whole[h][:, :DK] * keep
        ab_ref[h, :, DK:] = whole[h][:, DK:]


def local(head_order, block_starts, rim, hidden, w, conv_weight, log_decay, beta_rate):
    count = hidden.shape[0]
    smem, vmem = pl.BlockSpec(memory_space=pltpu.SMEM), pl.BlockSpec(memory_space=pltpu.VMEM)
    return pl.pallas_call(
        local_kernel,
        out_shape=(
            jax.ShapeDtypeStruct((2, DK, 2 * DK), F32),
            jax.ShapeDtypeStruct((2, count, DK), F32),
            jax.ShapeDtypeStruct((2, count, DK), F32),
        ),
        in_specs=[smem, smem] + [vmem] * 6,
        out_specs=(vmem, vmem, vmem),
        scratch_shapes=[pltpu.VMEM((count + RIM, 4 * DK), F32)],
        compiler_params=pltpu.CompilerParams(vmem_limit_bytes=48 << 20),
    )(head_order, block_starts, rim, hidden, w, conv_weight, log_decay, beta_rate)


def joined(later, earlier):
    both = mm(split(later[:, :DK]), split(earlier))
    return jnp.concatenate([both[:, :DK], both[:, DK:] + later[:, DK:]], axis=1)


def scan_kernel(
    n, ab_ref, reach_ref, inner_ref, gain_ref, out_ref,
    blocks, chips, lower, total, ring, acc, came, goes, states, sends, recvs, ring_send, ring_recv, line_send, line_recv,
):
    me, head = lax.axis_index("ctx"), lax.axis_index("head")
    chip, core = me // 2, lax.rem(me, 2)
    place = lax.rem(chip, QUAD)
    quad = chip // QUAD
    quads = n // (2 * QUAD)
    half = quads // 2
    upper = quad >= half
    side = lax.rem(chip, 2)
    rows = DK // CHUNKS
    top = place == QUAD - 1

    def at(z, c):
        return (z * 2 + c, head)

    mate = at(chip, 1 - core)
    other = at(chip + 1 - 2 * side, core)
    crown = at(quad * QUAD + QUAD - 1, core)
    base = quad * QUAD
    onward, behind = at(chip + QUAD, core), at(chip - QUAD, core)

    barrier = pltpu.get_barrier_semaphore()

    def greet(device):
        pl.semaphore_signal(barrier, inc=1, device_id=device, device_id_type=MESH)

    greet(mate)
    greet(other)

    @pl.when(place < 2)
    def _():
        greet(crown)

    @pl.when(top)
    def _():
        greet(at(base, core))
        greet(at(base + 1, core))

    @pl.when(top & (quad > 0))
    def _():
        greet(behind)

    @pl.when(top & (quad < quads - 1))
    def _():
        greet(onward)

    is_top = place // (QUAD - 1)
    beside = (quad + quads - 1) // quads + 1 - (quad + 1) // quads
    pl.semaphore_wait(barrier, 2 + 1 - place // 2 + is_top * (2 + beside))

    def copy(k, source, target, device):
        return pltpu.make_async_remote_copy(
            src_ref=source, dst_ref=target, send_sem=sends.at[k], recv_sem=recvs.at[k], device_id=device, device_id_type=MESH
        )

    first = copy(0, ab_ref.at[1 - core], blocks.at[core], mate)
    first.start()
    blocks[core] = ab_ref[core]
    first.wait_recv()
    chips[side] = joined(blocks[1], blocks[0])
    second = copy(1, chips.at[side], chips.at[side], other)
    second.start()
    second.wait_recv()

    rise = copy(2, total, lower, crown)

    @pl.when((place == 1) | top)
    def _():
        total[...] = joined(chips[1], chips[0])

    @pl.when(place == 1)
    def _():
        rise.start()

    def hop(step, part):
        span = pl.ds(part * rows, rows)
        return pltpu.make_async_remote_copy(
            src_ref=total.at[span] if step == 0 else ring.at[step - 1, span],
            dst_ref=ring.at[step, span],
            send_sem=ring_send.at[step, part],
            recv_sem=ring_recv.at[step, part],
            device_id=onward,
            device_id_type=MESH,
        )

    def pass_on(source, part):
        span = pl.ds(part * (DK // PARTS), DK // PARTS)
        return pltpu.make_async_remote_copy(
            src_ref=source.at[span],
            dst_ref=came.at[span],
            send_sem=line_send.at[part],
            recv_sem=line_recv.at[part],
            device_id=onward,
            device_id_type=MESH,
        )

    def given(k, target):
        return copy(3 + k, states.at[0 if k < 2 else 1], states.at[0], target)

    @pl.when(top)
    def _():
        rise.wait_recv()
        total[...] = joined(total[...], lower[...])

        @pl.when(upper & (quad < quads - 1))
        def _():
            for part in range(CHUNKS):
                hop(0, part).start()

        for step in range(quads - half - 1):

            @pl.when(quad - half > step)
            def _():
                for part in range(CHUNKS):
                    hop(step, part).wait_recv()
                    if step < quads - half - 2:

                        @pl.when(quad < quads - 1)
                        def _():
                            hop(step + 1, part).start()

                acc[...] = ring[0] if step == 0 else joined(acc[...], ring[step])

        @pl.when(quad == 0)
        def _():
            came[...] = jnp.zeros_like(came)

        @pl.when(quad > 0)
        def _():
            for part in range(PARTS):
                pass_on(came, part).wait_recv()

                @pl.when(upper & (quad < quads - 1))
                def _():
                    pass_on(came, part).start()

        @pl.when(quad < half)
        def _():
            goes[...] = mm(split(total[:, :DK]), split(came[...])) + total[:, DK:]
            for part in range(PARTS):
                pass_on(goes, part).start()

        @pl.when(quad <= half)
        def _():
            states[0] = came[...]

        @pl.when(quad > half)
        def _():
            states[0] = mm(split(acc[:, :DK]), split(came[...])) + acc[:, DK:]

        given(0, at(base, core)).start()
        given(1, at(base + 1, core)).start()
        states[1] = mm(split(lower[:, :DK]), split(states[0])) + lower[:, DK:]
        given(2, at(base + 2, core)).start()
        states[2] = mm(split(chips[0, :, :DK]), split(states[1])) + chips[0, :, DK:]

    for k in range(3):

        @pl.when(place == k)
        def _():
            given(k, crown).wait_recv()

    @pl.when((place == 0) | (place == 2))
    def _():
        states[2] = states[0]

    @pl.when(place == 1)
    def _():
        states[2] = mm(split(chips[0, :, :DK]), split(states[0])) + chips[0, :, DK:]

    states[3] = mm(split(blocks[0, :, :DK]), split(states[2])) + blocks[0, :, DK:]
    fifth = copy(6, states.at[3 - core], states.at[4], mate)
    fifth.start()

    def read(h, state):
        reads = inner_ref[h] + mm(split(reach_ref[h]), split(state))
        scaled = reads * lax.rsqrt(jnp.mean(reads * reads, axis=-1, keepdims=True) + eps) * gain_ref[...]
        out_ref[:, pl.ds(pl.multiple_of(h * DK, DK), DK)] = scaled.astype(BF16)

    read(core, states[2 + core])
    fifth.wait_recv()
    read(1 - core, states[4])
    for sent in (first, second, fifth):
        sent.wait_send()

    @pl.when(place == 1)
    def _():
        rise.wait_send()

    @pl.when(top)
    def _():
        for k in range(3):
            given(k, at(base + k, core)).wait_send()

    @pl.when(top & (quad < quads - 1))
    def _():
        for part in range(PARTS):
            pass_on(goes, part).wait_send()

    for step in range(quads - half - 1):

        @pl.when(top & (quad < quads - 1) & (quad - half >= step))
        def _():
            for part in range(CHUNKS):
                hop(step, part).wait_send()


def read_out(ab, reach, inner, norm_gain, n):
    quads = n // (2 * QUAD)
    steps = max(quads - quads // 2 - 1, 1)
    count = reach.shape[1]
    vmem = pl.BlockSpec(memory_space=pltpu.VMEM)
    dma = pltpu.SemaphoreType.DMA
    pair = pltpu.VMEM((2, DK, 2 * DK), F32)
    one = pltpu.VMEM((DK, 2 * DK), F32)
    state = pltpu.VMEM((DK, DK), F32)
    return pl.pallas_call(
        functools.partial(scan_kernel, n),
        out_shape=jax.ShapeDtypeStruct((count, 2 * DK), BF16),
        in_specs=[vmem] * 4,
        out_specs=vmem,
        scratch_shapes=[
            pair, pair, one, one, pltpu.VMEM((steps, DK, 2 * DK), F32), one, state, state,
            pltpu.VMEM((5, DK, DK), F32), dma((7,)), dma((7,)), dma((steps, CHUNKS)), dma((steps, CHUNKS)),
            dma((PARTS,)), dma((PARTS,)),
        ],
        compiler_params=pltpu.CompilerParams(collective_id=0, has_side_effects=True, vmem_limit_bytes=32 << 20),
    )(ab, reach, inner, norm_gain.reshape(1, DK))


def per_device(
    hidden,
    w_query,
    w_key,
    payload_projection_matrix,
    conv_weight,
    log_decay,
    beta_rate,
    norm_gain,
    head_order,
    block_starts,
):
    w, rim = exchange(head_order, w_query, w_key, payload_projection_matrix, hidden)
    ab, reach, inner = local(head_order, block_starts, rim, hidden, w, conv_weight, log_decay, beta_rate)
    return read_out(ab, reach, inner, norm_gain, lax.axis_size("ctx"))


def solution(mesh):
    return jax.shard_map(
        per_device,
        mesh=mesh,
        in_specs=(
            P("ctx", None),
            P("head", None),
            P("head", None),
            P("head", None),
            P(),
            P("head", "ctx"),
            P("head", "ctx"),
            P(),
            P(),
            P("ctx"),
        ),
        out_specs=P("ctx", "head"),
        check_vma=False,
    )
```

```python
import functools

import jax
import jax.numpy as jnp
from jax import lax
from jax.experimental import pallas as pl
from jax.experimental.pallas import tpu as pltpu
from jax.sharding import PartitionSpec as P

DK = 128
VALUE_HEAD_SIZE = 128
KCONV = 4
GROUP = 64
RIM = 16
SIDE = 4
CHUNKS = 4
QUAD = 4
PARTS = 2

MESH = pl.DeviceIdType.MESH
HIGH_PRECISION = lax.Precision.HIGHEST
F32 = jnp.float32
BF16 = jnp.bfloat16
eps = 1e-06


def split(a):
    high = a.astype(BF16)
    return high, (a - high.astype(F32)).astype(BF16)


def mm(a, b, left=1, right=0):
    def dot(x, y):
        return lax.dot_general(x, y, (((left,), (right,)), ((), ())), preferred_element_type=F32)

    return dot(a[0], b[0]) + (dot(a[0], b[1]) + dot(a[1], b[0]))


def exact(a, b, left=1, right=0):
    return lax.dot_general(
        a, b, (((left,), (right,)), ((), ())), precision=HIGH_PRECISION, preferred_element_type=F32
    )


def joined(later, earlier):
    both = mm(split(later[:, :DK]), split(earlier))
    return jnp.concatenate([both[:, :DK], both[:, DK:] + later[:, DK:]], axis=1)


def kernel(
    n, order_ref, starts_ref, query_ref, key_ref, value_ref, hidden_ref, conv_ref, decay_ref, beta_ref, gain_ref, out_ref,
    query, key, value, stage, w, ext, tap, proj, ab, reach, inner,
    blocks, chips, lower, total, ring, acc, came, goes, states,
    load_sem, send_sem, recv_sem, pass_send, pass_recv, rim_sem, local_sem,
    sends, recvs, ring_send, ring_recv, line_send, line_recv,
):
    me, head = lax.axis_index("ctx"), lax.axis_index("head")
    heads = lax.axis_size("head")
    chip, core = me // 2, lax.rem(me, 2)
    x, y = head // SIDE, lax.rem(head, SIDE)
    shard = query_ref.shape[0]
    half = shard // 2
    count = hidden_ref.shape[0]
    mine = pl.ds(pl.multiple_of(core * half, half), half)
    loads = []
    for j in range(heads):
        narrow, wide = pl.ds(j * DK, DK), pl.ds(2 * j * DK, 2 * DK)
        for i, (source, columns, target) in enumerate(
            ((query_ref, narrow, query), (key_ref, narrow, key), (value_ref, wide, value))
        ):
            loads.append(pltpu.make_async_copy(source.at[mine, columns], target.at[j], load_sem.at[i, j]))

    for load in loads:
        load.start()
    body = pltpu.make_async_copy(hidden_ref, ext.at[pl.ds(RIM, count)], local_sem.at[1])
    body.start()

    def peer(dx, dy):
        return lax.rem(x + dx, SIDE) * SIDE + lax.rem(y + dy, SIDE)

    offsets = sorted(
        ((dx, dy) for dx in range(SIDE) for dy in range(SIDE)),
        key=lambda o: (-(min(o[0], SIDE - o[0]) + min(o[1], SIDE - o[1])), o),
    )[: heads - 1]
    mate = (chip * 2 + 1 - core, head)
    following = (lax.rem(me + 1, n), head)
    previous = (lax.rem(me + n - 1, n), head)
    barrier = pltpu.get_barrier_semaphore()
    for device in [(me, peer(dx, dy)) for dx, dy in offsets] + [mate]:
        pl.semaphore_signal(barrier, inc=1, device_id=device, device_id_type=MESH)

    @pl.when(me > 0)
    def _():
        pl.semaphore_signal(barrier, inc=1, device_id=previous, device_id_type=MESH)

    place = lax.rem(chip, QUAD)
    quad = chip // QUAD
    quads = n // (2 * QUAD)
    middle = quads // 2
    upper = quad >= middle
    side = lax.rem(chip, 2)
    rows = DK // CHUNKS
    top = place == QUAD - 1

    def at(z, c):
        return (z * 2 + c, head)

    other = at(chip + 1 - 2 * side, core)
    crown = at(quad * QUAD + QUAD - 1, core)
    base = quad * QUAD
    onward, behind = at(chip + QUAD, core), at(chip - QUAD, core)

    def greet(device):
        pl.semaphore_signal(barrier, inc=1, device_id=device, device_id_type=MESH)

    greet(other)

    @pl.when(place < 2)
    def _():
        greet(crown)

    @pl.when(top)
    def _():
        greet(at(base, core))
        greet(at(base + 1, core))

    @pl.when(top & (quad > 0))
    def _():
        greet(behind)

    @pl.when(top & (quad < quads - 1))
    def _():
        greet(onward)

    def prepare(k, serve):
        logical = order_ref[serve]
        stage[k, :, :DK] = query[logical]
        stage[k, :, DK : 2 * DK] = key[logical]
        stage[k, :, 2 * DK :] = value[logical]

    for load in loads:
        load.wait()
    last = heads - 1
    for k, (dx, dy) in enumerate(offsets):
        prepare(k, peer(dx, dy))
    prepare(last, head)
    is_top = place // (QUAD - 1)
    beside = (quad + quads - 1) // quads + 1 - (quad + 1) // quads
    pl.semaphore_wait(barrier, heads + 1 - (me + 1) // n + 1 + 1 - place // 2 + is_top * (2 + beside))
    for j in range(tap.shape[0]):
        tap[j] = conv_ref[:, j * DK : (j + 1) * DK].astype(F32)


    rim = pltpu.make_async_remote_copy(
        src_ref=hidden_ref.at[pl.ds(count - RIM, RIM)],
        dst_ref=ext.at[pl.ds(0, RIM)],
        send_sem=rim_sem.at[0],
        recv_sem=rim_sem.at[1],
        device_id=following,
        device_id_type=MESH,
    )

    @pl.when(me < n - 1)
    def _():
        rim.start()

    def rows_of(source):
        return pl.ds(pl.multiple_of(source * shard + core * half, half), half)

    sent = []
    for k, (dx, dy) in enumerate(offsets):
        target = peer(dx, dy)
        copy = pltpu.make_async_remote_copy(
            src_ref=stage.at[k],
            dst_ref=w.at[rows_of(head)],
            send_sem=send_sem.at[k],
            recv_sem=recv_sem.at[k],
            device_id=(me, target),
            device_id_type=MESH,
        )
        copy.start()
        sent.append(copy)
    own = pltpu.make_async_copy(stage.at[last], w.at[rows_of(head)], local_sem.at[0])
    own.start()

    def passing(k, source, source_ref):
        return pltpu.make_async_remote_copy(
            src_ref=source_ref,
            dst_ref=w.at[rows_of(source)],
            send_sem=pass_send.at[k],
            recv_sem=pass_recv.at[k],
            device_id=mate,
            device_id_type=MESH,
        )

    passed = [passing(last, head, stage.at[last])]
    passed[0].start()
    for k in reversed(range(last)):
        dx, dy = offsets[k]
        source = peer(SIDE - dx, SIDE - dy)
        sent[k].wait_recv()
        copy = passing(k, source, w.at[rows_of(source)])
        copy.start()
        passed.append(copy)
    own.wait()
    body.wait()
    for copy in passed:
        copy.wait_recv()

    @pl.when(me > 0)
    def _():
        rim.wait_recv()

    @pl.when(me == 0)
    def _():
        ext[:RIM] = jnp.zeros((RIM, ext.shape[1]), BF16)

    groups = count // GROUP
    logical = order_ref[head]
    keep = jnp.where(starts_ref[0] == 0, 1.0, 0.0).astype(F32)
    edge = jnp.where(me > 0, keep, 0.0)
    raw = jnp.dot(ext[...], w[...], preferred_element_type=F32).astype(BF16).astype(F32)
    proj[RIM:] = raw[RIM:]
    proj[:RIM] = jnp.where(edge > 0.0, raw[:RIM], 0.0)

    def act(column, at_taps):
        taps = tap[at_taps]
        columns = slice(column, column + DK)
        total = taps[KCONV - 1 : KCONV] * proj[RIM:, columns]
        for lag in range(1, KCONV):
            at = KCONV - 1 - lag
            total = total + taps[at : at + 1] * proj[RIM - lag : RIM - lag + count, columns]
        return total / (1.0 + jnp.exp(-total))

    def unit(values):
        return values * lax.rsqrt(jnp.sum(values * values, axis=-1, keepdims=True) + eps)

    keys = unit(act(DK, heads + logical))
    queries = unit(act(0, logical))
    values = [act((2 + h) * DK, 2 * heads + 2 * logical + h) for h in range(2)]

    decay, beta = decay_ref[...], beta_ref[...]
    row = lax.broadcasted_iota(jnp.int32, (count, count), 0)
    col = lax.broadcasted_iota(jnp.int32, (count, count), 1)
    within = ((col <= row) & (col // GROUP == row // GROUP)).astype(F32)
    sums = exact(within, decay, 1, 1)
    strength = exact((row == col).astype(F32), beta, 1, 1)
    token = lax.broadcasted_iota(jnp.int32, (count, GROUP), 0)
    slot = lax.broadcasted_iota(jnp.int32, (count, GROUP), 1)

    r = lax.broadcasted_iota(jnp.int32, (GROUP, GROUP), 0)
    c = lax.broadcasted_iota(jnp.int32, (GROUP, GROUP), 1)
    eye = (r == c).astype(F32)
    eye_k = (
        lax.broadcasted_iota(jnp.int32, (DK, DK), 0) == lax.broadcasted_iota(jnp.int32, (DK, DK), 1)
    ).astype(F32)

    def below(size):
        return (r // (2 * size) == c // (2 * size)) & (r // size != c // size) & (c < r)

    tasks = []
    for g in range(groups):
        span = slice(g * GROUP, (g + 1) * GROUP)
        along = exact(decay, ((token // GROUP == g) & (token - g * GROUP <= slot)).astype(F32))
        k_g, q_g = keys[span], queries[span]
        k_s, q_s = split(k_g), split(q_g)
        key_key, query_key = mm(k_s, k_s, 1, 1), mm(q_s, k_s, 1, 1)
        for h in range(2):
            down = sums[span, h : h + 1]
            b = strength[span, h : h + 1]
            spread = jnp.exp(jnp.where(c <= r, down - along[h : h + 1], 0.0))
            system = jnp.where(c < r, b * spread * key_key, 0.0)
            attend = jnp.where(c <= r, spread * query_key, 0.0)
            grown = jnp.exp(down)
            end = down[GROUP - 1 : GROUP]
            tasks.append(
                dict(
                    h=h, g=g, system=system, attend=split(attend), q=grown * q_g, end=jnp.exp(end),
                    right=split(jnp.concatenate([b * values[h][span], (b * grown) * k_g], axis=1)),
                    trailing=split(jnp.exp(end - down) * k_g),
                    inverse=eye - jnp.where(below(1), system, 0.0),
                )
            )
    size = 2
    while size < GROUP:
        mask = below(size)
        for t in tasks:
            t["split"] = split(t["inverse"])
            t["half"] = mm(split(jnp.where(mask, t["system"], 0.0)), t["split"])
        for t in tasks:
            t["inverse"] = t["inverse"] - mm(t["split"], split(t["half"]))
        size *= 2
    for t in tasks:
        t["writes"] = split(mm(split(t["inverse"]), t["right"]))
    for t in tasks:
        seen = mm(t["attend"], t["writes"])
        t["inner"] = seen[:, :DK]
        t["reach"] = t["q"] - seen[:, DK:]
        moved = mm(t["trailing"], t["writes"], 0, 0)
        t["a"] = t["end"] * eye_k - moved[:, DK:]
        t["b"] = moved[:, :DK]
    whole = [None, None]
    for t in tasks:
        h, span = t["h"], slice(t["g"] * GROUP, (t["g"] + 1) * GROUP)
        if t["g"] == 0:
            reach[h, span] = t["reach"] * keep
            inner[h, span] = t["inner"]
            whole[h] = jnp.concatenate([t["a"], t["b"]], axis=1)
        else:
            entering = split(whole[h])
            both = mm(split(t["reach"]), entering)
            reach[h, span] = both[:, :DK] * keep
            inner[h, span] = t["inner"] + both[:, DK:]
            step = mm(split(t["a"]), entering)
            whole[h] = jnp.concatenate([step[:, :DK], step[:, DK:] + t["b"]], axis=1)
    for h in range(2):
        ab[h, :, :DK] = whole[h][:, :DK] * keep
        ab[h, :, DK:] = whole[h][:, DK:]

    def between(k, source, target, device):
        return pltpu.make_async_remote_copy(
            src_ref=source, dst_ref=target, send_sem=sends.at[k], recv_sem=recvs.at[k], device_id=device, device_id_type=MESH
        )

    first = between(0, ab.at[1 - core], blocks.at[core], mate)
    first.start()
    blocks[core] = ab[core]
    first.wait_recv()
    chips[side] = joined(blocks[1], blocks[0])
    second = between(1, chips.at[side], chips.at[side], other)
    second.start()
    second.wait_recv()

    rise = between(2, total, lower, crown)

    @pl.when((place == 1) | top)
    def _():
        total[...] = joined(chips[1], chips[0])

    @pl.when(place == 1)
    def _():
        rise.start()

    def hop(step, part):
        span = pl.ds(part * rows, rows)
        return pltpu.make_async_remote_copy(
            src_ref=total.at[span] if step == 0 else ring.at[step - 1, span],
            dst_ref=ring.at[step, span],
            send_sem=ring_send.at[step, part],
            recv_sem=ring_recv.at[step, part],
            device_id=onward,
            device_id_type=MESH,
        )

    def pass_on(source, part):
        span = pl.ds(part * (DK // PARTS), DK // PARTS)
        return pltpu.make_async_remote_copy(
            src_ref=source.at[span],
            dst_ref=came.at[span],
            send_sem=line_send.at[part],
            recv_sem=line_recv.at[part],
            device_id=onward,
            device_id_type=MESH,
        )

    def given(k, target):
        return between(3 + k, states.at[0 if k < 2 else 1], states.at[0], target)

    @pl.when(top)
    def _():
        rise.wait_recv()
        total[...] = joined(total[...], lower[...])

        @pl.when(upper & (quad < quads - 1))
        def _():
            for part in range(CHUNKS):
                hop(0, part).start()

        for step in range(quads - middle - 1):

            @pl.when(quad - middle > step)
            def _():
                for part in range(CHUNKS):
                    hop(step, part).wait_recv()
                    if step < quads - middle - 2:

                        @pl.when(quad < quads - 1)
                        def _():
                            hop(step + 1, part).start()

                acc[...] = ring[0] if step == 0 else joined(acc[...], ring[step])

        @pl.when(quad == 0)
        def _():
            came[...] = jnp.zeros_like(came)

        @pl.when(quad > 0)
        def _():
            for part in range(PARTS):
                pass_on(came, part).wait_recv()

                @pl.when(upper & (quad < quads - 1))
                def _():
                    pass_on(came, part).start()

        @pl.when(quad < middle)
        def _():
            goes[...] = mm(split(total[:, :DK]), split(came[...])) + total[:, DK:]
            for part in range(PARTS):
                pass_on(goes, part).start()

        @pl.when(quad <= middle)
        def _():
            states[0] = came[...]

        @pl.when(quad > middle)
        def _():
            states[0] = mm(split(acc[:, :DK]), split(came[...])) + acc[:, DK:]

        given(0, at(base, core)).start()
        given(1, at(base + 1, core)).start()
        states[1] = mm(split(lower[:, :DK]), split(states[0])) + lower[:, DK:]
        given(2, at(base + 2, core)).start()
        states[2] = mm(split(chips[0, :, :DK]), split(states[1])) + chips[0, :, DK:]

    for k in range(3):

        @pl.when(place == k)
        def _():
            given(k, crown).wait_recv()

    @pl.when((place == 0) | (place == 2))
    def _():
        states[2] = states[0]

    @pl.when(place == 1)
    def _():
        states[2] = mm(split(chips[0, :, :DK]), split(states[0])) + chips[0, :, DK:]

    states[3] = mm(split(blocks[0, :, :DK]), split(states[2])) + blocks[0, :, DK:]
    fifth = between(6, states.at[3 - core], states.at[4], mate)
    fifth.start()

    def read(h, state):
        reads = inner[h] + mm(split(reach[h]), split(state))
        scaled = reads * lax.rsqrt(jnp.mean(reads * reads, axis=-1, keepdims=True) + eps) * gain_ref[...]
        out_ref[:, pl.ds(pl.multiple_of(h * DK, DK), DK)] = scaled.astype(BF16)

    read(core, states[2 + core])
    fifth.wait_recv()
    read(1 - core, states[4])
    for done in (first, second, fifth):
        done.wait_send()

    @pl.when(place == 1)
    def _():
        rise.wait_send()

    @pl.when(top)
    def _():
        for k in range(3):
            given(k, at(base + k, core)).wait_send()

    @pl.when(top & (quad < quads - 1))
    def _():
        for part in range(PARTS):
            pass_on(goes, part).wait_send()

    for step in range(quads - middle - 1):

        @pl.when(top & (quad < quads - 1) & (quad - middle >= step))
        def _():
            for part in range(CHUNKS):
                hop(step, part).wait_send()
    for copy in sent + passed:
        copy.wait_send()

    @pl.when(me < n - 1)
    def _():
        rim.wait_send()


def per_device(
    hidden,
    w_query,
    w_key,
    payload_projection_matrix,
    conv_weight,
    log_decay,
    beta_rate,
    norm_gain,
    head_order,
    block_starts,
):
    n, heads = lax.axis_size("ctx"), lax.axis_size("head")
    (count, model), shard = hidden.shape, w_query.shape[0]
    half, width = shard // 2, 4 * DK
    quads = n // (2 * QUAD)
    steps = max(quads - quads // 2 - 1, 1)
    hbm = pl.BlockSpec(memory_space=pl.ANY)
    smem, vmem = pl.BlockSpec(memory_space=pltpu.SMEM), pl.BlockSpec(memory_space=pltpu.VMEM)
    dma = pltpu.SemaphoreType.DMA
    pair = pltpu.VMEM((2, DK, 2 * DK), F32)
    one = pltpu.VMEM((DK, 2 * DK), F32)
    state = pltpu.VMEM((DK, DK), F32)
    rows = pltpu.VMEM((2, count, DK), F32)
    return pl.pallas_call(
        functools.partial(kernel, n),
        out_shape=jax.ShapeDtypeStruct((count, 2 * DK), BF16),
        in_specs=[smem, smem] + [hbm] * 4 + [vmem] * 4,
        out_specs=vmem,
        scratch_shapes=[
            pltpu.VMEM((heads, half, DK), BF16),
            pltpu.VMEM((heads, half, DK), BF16),
            pltpu.VMEM((heads, half, 2 * DK), BF16),
            pltpu.VMEM((heads, half, width), BF16),
            pltpu.VMEM((heads * shard, width), BF16),
            pltpu.VMEM((count + RIM, model), BF16),
            pltpu.VMEM((4 * heads, KCONV, DK), F32),
            pltpu.VMEM((count + RIM, width), F32),
            pair, rows, rows,
            pair, pair, one, one, pltpu.VMEM((steps, DK, 2 * DK), F32), one, state, state,
            pltpu.VMEM((5, DK, DK), F32),
            dma((3, heads)), dma((heads,)), dma((heads,)), dma((heads,)), dma((heads,)), dma((2,)), dma((2,)),
            dma((7,)), dma((7,)), dma((steps, CHUNKS)), dma((steps, CHUNKS)), dma((PARTS,)), dma((PARTS,)),
        ],
        compiler_params=pltpu.CompilerParams(collective_id=0, has_side_effects=True, vmem_limit_bytes=56 << 20),
    )(
        head_order, block_starts, w_query, w_key, payload_projection_matrix, hidden, conv_weight, log_decay, beta_rate,
        norm_gain.reshape(1, DK),
    )


def solution(mesh):
    return jax.shard_map(
        per_device,
        mesh=mesh,
        in_specs=(
            P("ctx", None),
            P("head", None),
            P("head", None),
            P("head", None),
            P(),
            P("head", "ctx"),
            P("head", "ctx"),
            P(),
            P(),
            P("ctx"),
        ),
        out_specs=P("ctx", "head"),
        check_vma=False,
    )
```

```python
import functools

import jax
import jax.numpy as jnp
from jax import lax
from jax.experimental import pallas as pl
from jax.experimental.pallas import tpu as pltpu
from jax.sharding import PartitionSpec as P

DK = 128
VALUE_HEAD_SIZE = 128
KCONV = 4
GROUP = 64
RIM = 16
SIDE = 4
CHUNKS = 4
QUAD = 4

MESH = pl.DeviceIdType.MESH
HIGH_PRECISION = lax.Precision.HIGHEST
F32 = jnp.float32
BF16 = jnp.bfloat16
eps = 1e-06


def split(a):
    high = a.astype(BF16)
    return high, (a - high.astype(F32)).astype(BF16)


def mm(a, b, left=1, right=0):
    def dot(x, y):
        return lax.dot_general(x, y, (((left,), (right,)), ((), ())), preferred_element_type=F32)

    return dot(a[0], b[0]) + (dot(a[0], b[1]) + dot(a[1], b[0]))


def exact(a, b, left=1, right=0):
    return lax.dot_general(
        a, b, (((left,), (right,)), ((), ())), precision=HIGH_PRECISION, preferred_element_type=F32
    )


def joined(later, earlier):
    both = mm(split(later[:, :DK]), split(earlier))
    return jnp.concatenate([both[:, :DK], both[:, DK:] + later[:, DK:]], axis=1)


def kernel(
    n, order_ref, starts_ref, query_ref, key_ref, value_ref, hidden_ref, conv_ref, decay_ref, beta_ref, gain_ref, out_ref,
    query, key, value, stage, w, ext, tap, proj, ab, reach, inner,
    blocks, chips, lower, total, ring, acc, came, goes, states,
    load_sem, send_sem, recv_sem, pass_send, pass_recv, rim_sem, local_sem,
    sends, recvs, ring_send, ring_recv, line_send, line_recv, clear,
):
    me, head = lax.axis_index("ctx"), lax.axis_index("head")
    heads = lax.axis_size("head")
    chip, core = me // 2, lax.rem(me, 2)
    x, y = head // SIDE, lax.rem(head, SIDE)
    shard = query_ref.shape[0]
    half = shard // 2
    count = hidden_ref.shape[0]
    mine = pl.ds(pl.multiple_of(core * half, half), half)
    loads = []
    for j in range(heads):
        narrow, wide = pl.ds(j * DK, DK), pl.ds(2 * j * DK, 2 * DK)
        for i, (source, columns, target) in enumerate(
            ((query_ref, narrow, query), (key_ref, narrow, key), (value_ref, wide, value))
        ):
            loads.append(pltpu.make_async_copy(source.at[mine, columns], target.at[j], load_sem.at[i, j]))

    for load in loads:
        load.start()
    body = pltpu.make_async_copy(hidden_ref, ext.at[pl.ds(RIM, count)], local_sem.at[1])
    body.start()

    def peer(dx, dy):
        return lax.rem(x + dx, SIDE) * SIDE + lax.rem(y + dy, SIDE)

    offsets = sorted(
        ((dx, dy) for dx in range(SIDE) for dy in range(SIDE)),
        key=lambda o: (-(min(o[0], SIDE - o[0]) + min(o[1], SIDE - o[1])), o),
    )[: heads - 1]
    mate = (chip * 2 + 1 - core, head)
    following = (lax.rem(me + 1, n), head)
    previous = (lax.rem(me + n - 1, n), head)
    barrier = pltpu.get_barrier_semaphore()
    for device in [(me, peer(dx, dy)) for dx, dy in offsets] + [mate]:
        pl.semaphore_signal(barrier, inc=1, device_id=device, device_id_type=MESH)

    @pl.when(me > 0)
    def _():
        pl.semaphore_signal(barrier, inc=1, device_id=previous, device_id_type=MESH)

    place = lax.rem(chip, QUAD)
    quad = chip // QUAD
    quads = n // (2 * QUAD)
    middle = quads // 2
    upper = quad >= middle
    side = lax.rem(chip, 2)
    rows = DK // CHUNKS
    top = place == QUAD - 1

    def at(z, c):
        return (z * 2 + c, head)

    other = at(chip + 1 - 2 * side, core)
    crown = at(quad * QUAD + QUAD - 1, core)
    base = quad * QUAD
    onward, behind = at(chip + QUAD, core), at(chip - QUAD, core)

    def greet(device):
        pl.semaphore_signal(barrier, inc=1, device_id=device, device_id_type=MESH)

    greet(other)

    @pl.when(place < 2)
    def _():
        greet(crown)

    @pl.when(top)
    def _():
        greet(at(base, core))
        greet(at(base + 1, core))

    @pl.when(top & (quad > 0))
    def _():
        greet(behind)

    @pl.when(top & (quad < quads - 1))
    def _():
        greet(onward)

    def prepare(k, serve):
        logical = order_ref[serve]
        stage[k, :, :DK] = query[logical]
        stage[k, :, DK : 2 * DK] = key[logical]
        stage[k, :, 2 * DK :] = value[logical]

    for load in loads:
        load.wait()
    last = heads - 1
    for k, (dx, dy) in enumerate(offsets):
        prepare(k, peer(dx, dy))
    prepare(last, head)
    is_top = place // (QUAD - 1)
    beside = (quad + quads - 1) // quads + 1 - (quad + 1) // quads
    pl.semaphore_wait(barrier, heads + 1 - (me + 1) // n + 1 + 1 - place // 2 + is_top * (2 + beside))

    @pl.when(top & (quad == quads - 1))
    def _():
        pl.semaphore_signal(clear, inc=1, device_id=behind, device_id_type=MESH)

    def relay(k):
        @pl.when(top & (quad == quads - 2 - k))
        def _():
            pl.semaphore_wait(clear, 1)
            pl.semaphore_signal(clear, inc=1, device_id=behind, device_id_type=MESH)

    relays = quads - 1 - middle

    for j in range(tap.shape[0]):
        tap[j] = conv_ref[:, j * DK : (j + 1) * DK].astype(F32)


    rim = pltpu.make_async_remote_copy(
        src_ref=hidden_ref.at[pl.ds(count - RIM, RIM)],
        dst_ref=ext.at[pl.ds(0, RIM)],
        send_sem=rim_sem.at[0],
        recv_sem=rim_sem.at[1],
        device_id=following,
        device_id_type=MESH,
    )

    @pl.when(me < n - 1)
    def _():
        rim.start()

    def rows_of(source):
        return pl.ds(pl.multiple_of(source * shard + core * half, half), half)

    sent = []
    for k, (dx, dy) in enumerate(offsets):
        target = peer(dx, dy)
        copy = pltpu.make_async_remote_copy(
            src_ref=stage.at[k],
            dst_ref=w.at[rows_of(head)],
            send_sem=send_sem.at[k],
            recv_sem=recv_sem.at[k],
            device_id=(me, target),
            device_id_type=MESH,
        )
        copy.start()
        sent.append(copy)
    own = pltpu.make_async_copy(stage.at[last], w.at[rows_of(head)], local_sem.at[0])
    own.start()

    def passing(k, source, source_ref):
        return pltpu.make_async_remote_copy(
            src_ref=source_ref,
            dst_ref=w.at[rows_of(source)],
            send_sem=pass_send.at[k],
            recv_sem=pass_recv.at[k],
            device_id=mate,
            device_id_type=MESH,
        )

    passed = [passing(last, head, stage.at[last])]
    passed[0].start()
    for k in reversed(range(last)):
        dx, dy = offsets[k]
        source = peer(SIDE - dx, SIDE - dy)
        sent[k].wait_recv()
        copy = passing(k, source, w.at[rows_of(source)])
        copy.start()
        passed.append(copy)
    own.wait()
    body.wait()
    for copy in passed:
        copy.wait_recv()

    @pl.when(me > 0)
    def _():
        rim.wait_recv()

    @pl.when(me == 0)
    def _():
        ext[:RIM] = jnp.zeros((RIM, ext.shape[1]), BF16)

    for k in range(min(1, relays)):
        relay(k)

    groups = count // GROUP
    logical = order_ref[head]
    keep = jnp.where(starts_ref[0] == 0, 1.0, 0.0).astype(F32)
    edge = jnp.where(me > 0, keep, 0.0)
    raw = jnp.dot(ext[...], w[...], preferred_element_type=F32).astype(BF16).astype(F32)
    proj[RIM:] = raw[RIM:]
    proj[:RIM] = jnp.where(edge > 0.0, raw[:RIM], 0.0)

    def act(column, at_taps):
        taps = tap[at_taps]
        columns = slice(column, column + DK)
        total = taps[KCONV - 1 : KCONV] * proj[RIM:, columns]
        for lag in range(1, KCONV):
            at = KCONV - 1 - lag
            total = total + taps[at : at + 1] * proj[RIM - lag : RIM - lag + count, columns]
        return total / (1.0 + jnp.exp(-total))

    def unit(values):
        return values * lax.rsqrt(jnp.sum(values * values, axis=-1, keepdims=True) + eps)

    keys = unit(act(DK, heads + logical))
    queries = unit(act(0, logical))
    values = [act((2 + h) * DK, 2 * heads + 2 * logical + h) for h in range(2)]

    decay, beta = decay_ref[...], beta_ref[...]
    row = lax.broadcasted_iota(jnp.int32, (count, count), 0)
    col = lax.broadcasted_iota(jnp.int32, (count, count), 1)
    within = ((col <= row) & (col // GROUP == row // GROUP)).astype(F32)
    sums = exact(within, decay, 1, 1)
    strength = exact((row == col).astype(F32), beta, 1, 1)
    token = lax.broadcasted_iota(jnp.int32, (count, GROUP), 0)
    slot = lax.broadcasted_iota(jnp.int32, (count, GROUP), 1)

    r = lax.broadcasted_iota(jnp.int32, (GROUP, GROUP), 0)
    c = lax.broadcasted_iota(jnp.int32, (GROUP, GROUP), 1)
    eye = (r == c).astype(F32)
    eye_k = (
        lax.broadcasted_iota(jnp.int32, (DK, DK), 0) == lax.broadcasted_iota(jnp.int32, (DK, DK), 1)
    ).astype(F32)

    def below(size):
        return (r // (2 * size) == c // (2 * size)) & (r // size != c // size) & (c < r)

    tasks = []
    for g in range(groups):
        span = slice(g * GROUP, (g + 1) * GROUP)
        along = exact(decay, ((token // GROUP == g) & (token - g * GROUP <= slot)).astype(F32))
        k_g, q_g = keys[span], queries[span]
        k_s, q_s = split(k_g), split(q_g)
        key_key, query_key = mm(k_s, k_s, 1, 1), mm(q_s, k_s, 1, 1)
        for h in range(2):
            down = sums[span, h : h + 1]
            b = strength[span, h : h + 1]
            spread = jnp.exp(jnp.where(c <= r, down - along[h : h + 1], 0.0))
            system = jnp.where(c < r, b * spread * key_key, 0.0)
            attend = jnp.where(c <= r, spread * query_key, 0.0)
            grown = jnp.exp(down)
            end = down[GROUP - 1 : GROUP]
            tasks.append(
                dict(
                    h=h, g=g, system=system, attend=split(attend), q=grown * q_g, end=jnp.exp(end),
                    right=split(jnp.concatenate([b * values[h][span], (b * grown) * k_g], axis=1)),
                    trailing=split(jnp.exp(end - down) * k_g),
                    inverse=eye - jnp.where(below(1), system, 0.0),
                )
            )
    size = 2
    while size < GROUP:
        mask = below(size)
        for t in tasks:
            t["split"] = split(t["inverse"])
            t["half"] = mm(split(jnp.where(mask, t["system"], 0.0)), t["split"])
        for t in tasks:
            t["inverse"] = t["inverse"] - mm(t["split"], split(t["half"]))
        size *= 2
    for t in tasks:
        t["writes"] = split(mm(split(t["inverse"]), t["right"]))
    for t in tasks:
        seen = mm(t["attend"], t["writes"])
        t["inner"] = seen[:, :DK]
        t["reach"] = t["q"] - seen[:, DK:]
        moved = mm(t["trailing"], t["writes"], 0, 0)
        t["a"] = t["end"] * eye_k - moved[:, DK:]
        t["b"] = moved[:, :DK]
    whole = [None, None]
    for t in tasks:
        h, span = t["h"], slice(t["g"] * GROUP, (t["g"] + 1) * GROUP)
        if t["g"] == 0:
            reach[h, span] = t["reach"] * keep
            inner[h, span] = t["inner"]
            whole[h] = jnp.concatenate([t["a"], t["b"]], axis=1)
        else:
            entering = split(whole[h])
            both = mm(split(t["reach"]), entering)
            reach[h, span] = both[:, :DK] * keep
            inner[h, span] = t["inner"] + both[:, DK:]
            step = mm(split(t["a"]), entering)
            whole[h] = jnp.concatenate([step[:, :DK], step[:, DK:] + t["b"]], axis=1)
    for h in range(2):
        ab[h, :, :DK] = whole[h][:, :DK] * keep
        ab[h, :, DK:] = whole[h][:, DK:]

    for k in range(1, min(2, relays)):
        relay(k)

    def between(k, source, target, device):
        return pltpu.make_async_remote_copy(
            src_ref=source, dst_ref=target, send_sem=sends.at[k], recv_sem=recvs.at[k], device_id=device, device_id_type=MESH
        )

    first = between(0, ab.at[1 - core], blocks.at[core], mate)
    first.start()
    blocks[core] = ab[core]
    first.wait_recv()
    chips[side] = joined(blocks[1], blocks[0])
    second = between(1, chips.at[side], chips.at[side], other)
    second.start()
    second.wait_recv()
    for k in range(2, relays):
        relay(k)

    rise = between(2, total, lower, crown)

    @pl.when((place == 1) | top)
    def _():
        total[...] = joined(chips[1], chips[0])

    @pl.when(place == 1)
    def _():
        rise.start()

    def hop(step, part):
        span = pl.ds(part * rows, rows)
        return pltpu.make_async_remote_copy(
            src_ref=total.at[span] if step == 0 else ring.at[step - 1, span],
            dst_ref=ring.at[step, span],
            send_sem=ring_send.at[step, part],
            recv_sem=ring_recv.at[step, part],
            device_id=onward,
            device_id_type=MESH,
        )

    def pass_on(k, device):
        return pltpu.make_async_remote_copy(
            src_ref=goes, dst_ref=came, send_sem=line_send.at[k], recv_sem=line_recv.at[0], device_id=device, device_id_type=MESH
        )

    def far(k):
        return pass_on(k, at(chip + QUAD * (k + 1), core))

    def given(k, target):
        return between(3 + k, states.at[0 if k < 2 else 1], states.at[0], target)

    @pl.when(top)
    def _():
        rise.wait_recv()
        total[...] = joined(total[...], lower[...])

        @pl.when(upper & (quad < quads - 1))
        def _():
            for part in range(CHUNKS):
                hop(0, part).start()

        for step in range(quads - middle - 1):

            @pl.when(quad - middle > step)
            def _():
                for part in range(CHUNKS):
                    hop(step, part).wait_recv()
                    if step < quads - middle - 2:

                        @pl.when(quad < quads - 1)
                        def _():
                            hop(step + 1, part).start()

                acc[...] = ring[0] if step == 0 else joined(acc[...], ring[step])

        @pl.when(quad == 0)
        def _():
            came[...] = jnp.zeros_like(came)

        @pl.when(quad > 0)
        def _():
            pass_on(0, onward).wait_recv()

        @pl.when(quad < middle)
        def _():
            goes[...] = mm(split(total[:, :DK]), split(came[...])) + total[:, DK:]

        @pl.when(quad < middle - 1)
        def _():
            pass_on(0, onward).start()

        @pl.when(quad == middle - 1)
        def _():
            pl.semaphore_wait(clear, 1)
            for k in reversed(range(quads - middle)):
                far(k).start()

        @pl.when(quad <= middle)
        def _():
            states[0] = came[...]

        @pl.when(quad > middle)
        def _():
            states[0] = mm(split(acc[:, :DK]), split(came[...])) + acc[:, DK:]

        given(0, at(base, core)).start()
        given(1, at(base + 1, core)).start()
        states[1] = mm(split(lower[:, :DK]), split(states[0])) + lower[:, DK:]
        given(2, at(base + 2, core)).start()
        states[2] = mm(split(chips[0, :, :DK]), split(states[1])) + chips[0, :, DK:]

    for k in range(3):

        @pl.when(place == k)
        def _():
            given(k, crown).wait_recv()

    @pl.when((place == 0) | (place == 2))
    def _():
        states[2] = states[0]

    @pl.when(place == 1)
    def _():
        states[2] = mm(split(chips[0, :, :DK]), split(states[0])) + chips[0, :, DK:]

    states[3] = mm(split(blocks[0, :, :DK]), split(states[2])) + blocks[0, :, DK:]
    fifth = between(6, states.at[3 - core], states.at[4], mate)
    fifth.start()

    def read(h, state):
        reads = inner[h] + mm(split(reach[h]), split(state))
        scaled = reads * lax.rsqrt(jnp.mean(reads * reads, axis=-1, keepdims=True) + eps) * gain_ref[...]
        out_ref[:, pl.ds(pl.multiple_of(h * DK, DK), DK)] = scaled.astype(BF16)

    read(core, states[2 + core])
    fifth.wait_recv()
    read(1 - core, states[4])
    for done in (first, second, fifth):
        done.wait_send()

    @pl.when(place == 1)
    def _():
        rise.wait_send()

    @pl.when(top)
    def _():
        for k in range(3):
            given(k, at(base + k, core)).wait_send()

    @pl.when(top & (quad < middle - 1))
    def _():
        pass_on(0, onward).wait_send()

    @pl.when(top & (quad == middle - 1))
    def _():
        for k in range(quads - middle):
            far(k).wait_send()

    for step in range(quads - middle - 1):

        @pl.when(top & (quad < quads - 1) & (quad - middle >= step))
        def _():
            for part in range(CHUNKS):
                hop(step, part).wait_send()
    for copy in sent + passed:
        copy.wait_send()

    @pl.when(me < n - 1)
    def _():
        rim.wait_send()


def per_device(
    hidden,
    w_query,
    w_key,
    payload_projection_matrix,
    conv_weight,
    log_decay,
    beta_rate,
    norm_gain,
    head_order,
    block_starts,
):
    n, heads = lax.axis_size("ctx"), lax.axis_size("head")
    (count, model), shard = hidden.shape, w_query.shape[0]
    half, width = shard // 2, 4 * DK
    quads = n // (2 * QUAD)
    steps = max(quads - quads // 2 - 1, 1)
    hbm = pl.BlockSpec(memory_space=pl.ANY)
    smem, vmem = pl.BlockSpec(memory_space=pltpu.SMEM), pl.BlockSpec(memory_space=pltpu.VMEM)
    dma = pltpu.SemaphoreType.DMA
    pair = pltpu.VMEM((2, DK, 2 * DK), F32)
    one = pltpu.VMEM((DK, 2 * DK), F32)
    state = pltpu.VMEM((DK, DK), F32)
    rows = pltpu.VMEM((2, count, DK), F32)
    return pl.pallas_call(
        functools.partial(kernel, n),
        out_shape=jax.ShapeDtypeStruct((count, 2 * DK), BF16),
        in_specs=[smem, smem] + [hbm] * 4 + [vmem] * 4,
        out_specs=vmem,
        scratch_shapes=[
            pltpu.VMEM((heads, half, DK), BF16),
            pltpu.VMEM((heads, half, DK), BF16),
            pltpu.VMEM((heads, half, 2 * DK), BF16),
            pltpu.VMEM((heads, half, width), BF16),
            pltpu.VMEM((heads * shard, width), BF16),
            pltpu.VMEM((count + RIM, model), BF16),
            pltpu.VMEM((4 * heads, KCONV, DK), F32),
            pltpu.VMEM((count + RIM, width), F32),
            pair, rows, rows,
            pair, pair, one, one, pltpu.VMEM((steps, DK, 2 * DK), F32), one, state, state,
            pltpu.VMEM((5, DK, DK), F32),
            dma((3, heads)), dma((heads,)), dma((heads,)), dma((heads,)), dma((heads,)), dma((2,)), dma((2,)),
            dma((7,)), dma((7,)), dma((steps, CHUNKS)), dma((steps, CHUNKS)), dma((quads - quads // 2,)), dma((1,)),
            pltpu.SemaphoreType.REGULAR,
        ],
        compiler_params=pltpu.CompilerParams(collective_id=0, has_side_effects=True, vmem_limit_bytes=56 << 20),
    )(
        head_order, block_starts, w_query, w_key, payload_projection_matrix, hidden, conv_weight, log_decay, beta_rate,
        norm_gain.reshape(1, DK),
    )


def solution(mesh):
    return jax.shard_map(
        per_device,
        mesh=mesh,
        in_specs=(
            P("ctx", None),
            P("head", None),
            P("head", None),
            P("head", None),
            P(),
            P("head", "ctx"),
            P("head", "ctx"),
            P(),
            P(),
            P("ctx"),
        ),
        out_specs=P("ctx", "head"),
        check_vma=False,
    )
```

```python
import functools

import jax
import jax.numpy as jnp
from jax import lax
from jax.experimental import pallas as pl
from jax.experimental.pallas import tpu as pltpu
from jax.sharding import PartitionSpec as P

DK = 128
VALUE_HEAD_SIZE = 128
KCONV = 4
GROUP = 64
RIM = 16
SIDE = 4
CHUNKS = 4
QUAD = 4

MESH = pl.DeviceIdType.MESH
HIGH_PRECISION = lax.Precision.HIGHEST
F32 = jnp.float32
BF16 = jnp.bfloat16
eps = 1e-06


def split(a):
    high = a.astype(BF16)
    return high, (a - high.astype(F32)).astype(BF16)


def mm(a, b, left=1, right=0):
    def dot(x, y):
        return lax.dot_general(x, y, (((left,), (right,)), ((), ())), preferred_element_type=F32)

    return dot(a[0], b[0]) + (dot(a[0], b[1]) + dot(a[1], b[0]))


def exact(a, b, left=1, right=0):
    return lax.dot_general(
        a, b, (((left,), (right,)), ((), ())), precision=HIGH_PRECISION, preferred_element_type=F32
    )


def joined(later, earlier):
    both = mm(split(later[:, :DK]), split(earlier))
    return jnp.concatenate([both[:, :DK], both[:, DK:] + later[:, DK:]], axis=1)


def kernel(
    n, order_ref, starts_ref, query_ref, key_ref, value_ref, hidden_ref, conv_ref, decay_ref, beta_ref, gain_ref, out_ref,
    query, key, value, stage, w, ext, tap, proj, ab, reach, inner,
    blocks, chips, lower, total, ring, acc, came, goes, states,
    load_sem, send_sem, recv_sem, pass_send, pass_recv, rim_sem, local_sem,
    sends, recvs, ring_send, ring_recv, line_send, line_recv, clear,
):
    me, head = lax.axis_index("ctx"), lax.axis_index("head")
    heads = lax.axis_size("head")
    chip, core = me // 2, lax.rem(me, 2)
    x, y = head // SIDE, lax.rem(head, SIDE)
    shard = query_ref.shape[0]
    half = shard // 2
    count = hidden_ref.shape[0]
    mine = pl.ds(pl.multiple_of(core * half, half), half)
    loads = []
    for j in range(heads):
        narrow, wide = pl.ds(j * DK, DK), pl.ds(2 * j * DK, 2 * DK)
        for i, (source, columns, target) in enumerate(
            ((query_ref, narrow, query), (key_ref, narrow, key), (value_ref, wide, value))
        ):
            loads.append(pltpu.make_async_copy(source.at[mine, columns], target.at[j], load_sem.at[i, j]))

    for load in loads:
        load.start()
    body = pltpu.make_async_copy(hidden_ref, ext.at[pl.ds(RIM, count)], local_sem.at[1])
    body.start()

    def peer(dx, dy):
        return lax.rem(x + dx, SIDE) * SIDE + lax.rem(y + dy, SIDE)

    offsets = sorted(
        ((dx, dy) for dx in range(SIDE) for dy in range(SIDE)),
        key=lambda o: (-(min(o[0], SIDE - o[0]) + min(o[1], SIDE - o[1])), o),
    )[: heads - 1]
    mate = (chip * 2 + 1 - core, head)
    following = (lax.rem(me + 1, n), head)
    previous = (lax.rem(me + n - 1, n), head)
    barrier = pltpu.get_barrier_semaphore()
    for device in [(me, peer(dx, dy)) for dx, dy in offsets] + [mate]:
        pl.semaphore_signal(barrier, inc=1, device_id=device, device_id_type=MESH)

    @pl.when(me > 0)
    def _():
        pl.semaphore_signal(barrier, inc=1, device_id=previous, device_id_type=MESH)

    place = lax.rem(chip, QUAD)
    quad = chip // QUAD
    quads = n // (2 * QUAD)
    middle = quads // 2
    upper = quad >= middle
    side = lax.rem(chip, 2)
    rows = DK // CHUNKS
    top = place == QUAD - 1

    def at(z, c):
        return (z * 2 + c, head)

    other = at(chip + 1 - 2 * side, core)
    crown = at(quad * QUAD + QUAD - 1, core)
    base = quad * QUAD
    onward, behind = at(chip + QUAD, core), at(chip - QUAD, core)

    def greet(device):
        pl.semaphore_signal(barrier, inc=1, device_id=device, device_id_type=MESH)

    greet(other)

    @pl.when(place < 2)
    def _():
        greet(crown)

    @pl.when(top)
    def _():
        greet(at(base, core))
        greet(at(base + 1, core))

    @pl.when(top & (quad > 0))
    def _():
        greet(behind)

    @pl.when(top & (quad < quads - 1))
    def _():
        greet(onward)

    def prepare(k, serve):
        logical = order_ref[serve]
        stage[k, :, :DK] = query[logical]
        stage[k, :, DK : 2 * DK] = key[logical]
        stage[k, :, 2 * DK :] = value[logical]

    for load in loads:
        load.wait()
    last = heads - 1
    for k, (dx, dy) in enumerate(offsets):
        prepare(k, peer(dx, dy))
    prepare(last, head)
    is_top = place // (QUAD - 1)
    beside = (quad + quads - 1) // quads + 1 - (quad + 1) // quads
    pl.semaphore_wait(barrier, heads + 1 - (me + 1) // n + 1 + 1 - place // 2 + is_top * (2 + beside))

    @pl.when(top & (quad == quads - 1))
    def _():
        pl.semaphore_signal(clear, inc=1, device_id=behind, device_id_type=MESH)

    def relay(k):
        @pl.when(top & (quad == quads - 2 - k))
        def _():
            pl.semaphore_wait(clear, 1)
            pl.semaphore_signal(clear, inc=1, device_id=behind, device_id_type=MESH)

    relays = quads - 1 - middle


    rim = pltpu.make_async_remote_copy(
        src_ref=hidden_ref.at[pl.ds(count - RIM, RIM)],
        dst_ref=ext.at[pl.ds(0, RIM)],
        send_sem=rim_sem.at[0],
        recv_sem=rim_sem.at[1],
        device_id=following,
        device_id_type=MESH,
    )

    @pl.when(me < n - 1)
    def _():
        rim.start()

    def rows_of(source):
        return pl.ds(pl.multiple_of(source * shard + core * half, half), half)

    sent = []
    for k, (dx, dy) in enumerate(offsets):
        target = peer(dx, dy)
        copy = pltpu.make_async_remote_copy(
            src_ref=stage.at[k],
            dst_ref=w.at[rows_of(head)],
            send_sem=send_sem.at[k],
            recv_sem=recv_sem.at[k],
            device_id=(me, target),
            device_id_type=MESH,
        )
        copy.start()
        sent.append(copy)
    own = pltpu.make_async_copy(stage.at[last], w.at[rows_of(head)], local_sem.at[0])
    own.start()

    def passing(k, source, source_ref):
        return pltpu.make_async_remote_copy(
            src_ref=source_ref,
            dst_ref=w.at[rows_of(source)],
            send_sem=pass_send.at[k],
            recv_sem=pass_recv.at[k],
            device_id=mate,
            device_id_type=MESH,
        )

    passed = [passing(last, head, stage.at[last])]
    passed[0].start()
    for j in range(tap.shape[0]):
        tap[j] = conv_ref[:, j * DK : (j + 1) * DK].astype(F32)
    for k in range(last):
        dx, dy = offsets[k]
        source = peer(SIDE - dx, SIDE - dy)
        sent[k].wait_recv()
        copy = passing(k, source, w.at[rows_of(source)])
        copy.start()
        passed.append(copy)
    own.wait()
    body.wait()
    for copy in passed:
        copy.wait_recv()

    @pl.when(me > 0)
    def _():
        rim.wait_recv()

    @pl.when(me == 0)
    def _():
        ext[:RIM] = jnp.zeros((RIM, ext.shape[1]), BF16)

    for k in range(min(1, relays)):
        relay(k)

    groups = count // GROUP
    logical = order_ref[head]
    keep = jnp.where(starts_ref[0] == 0, 1.0, 0.0).astype(F32)
    edge = jnp.where(me > 0, keep, 0.0)
    raw = jnp.dot(ext[...], w[...], preferred_element_type=F32).astype(BF16).astype(F32)
    proj[RIM:] = raw[RIM:]
    proj[:RIM] = jnp.where(edge > 0.0, raw[:RIM], 0.0)

    def act(column, at_taps):
        taps = tap[at_taps]
        columns = slice(column, column + DK)
        total = taps[KCONV - 1 : KCONV] * proj[RIM:, columns]
        for lag in range(1, KCONV):
            at = KCONV - 1 - lag
            total = total + taps[at : at + 1] * proj[RIM - lag : RIM - lag + count, columns]
        return total / (1.0 + jnp.exp(-total))

    def unit(values):
        return values * lax.rsqrt(jnp.sum(values * values, axis=-1, keepdims=True) + eps)

    keys = unit(act(DK, heads + logical))
    queries = unit(act(0, logical))
    values = [act((2 + h) * DK, 2 * heads + 2 * logical + h) for h in range(2)]

    decay, beta = decay_ref[...], beta_ref[...]
    row = lax.broadcasted_iota(jnp.int32, (count, count), 0)
    col = lax.broadcasted_iota(jnp.int32, (count, count), 1)
    within = ((col <= row) & (col // GROUP == row // GROUP)).astype(F32)
    sums = exact(within, decay, 1, 1)
    strength = exact((row == col).astype(F32), beta, 1, 1)
    token = lax.broadcasted_iota(jnp.int32, (count, GROUP), 0)
    slot = lax.broadcasted_iota(jnp.int32, (count, GROUP), 1)

    r = lax.broadcasted_iota(jnp.int32, (GROUP, GROUP), 0)
    c = lax.broadcasted_iota(jnp.int32, (GROUP, GROUP), 1)
    eye = (r == c).astype(F32)
    eye_k = (
        lax.broadcasted_iota(jnp.int32, (DK, DK), 0) == lax.broadcasted_iota(jnp.int32, (DK, DK), 1)
    ).astype(F32)

    def below(size):
        return (r // (2 * size) == c // (2 * size)) & (r // size != c // size) & (c < r)

    tasks = []
    for g in range(groups):
        span = slice(g * GROUP, (g + 1) * GROUP)
        along = exact(decay, ((token // GROUP == g) & (token - g * GROUP <= slot)).astype(F32))
        k_g, q_g = keys[span], queries[span]
        k_s, q_s = split(k_g), split(q_g)
        key_key, query_key = mm(k_s, k_s, 1, 1), mm(q_s, k_s, 1, 1)
        for h in range(2):
            down = sums[span, h : h + 1]
            b = strength[span, h : h + 1]
            spread = jnp.exp(jnp.where(c <= r, down - along[h : h + 1], 0.0))
            system = jnp.where(c < r, b * spread * key_key, 0.0)
            attend = jnp.where(c <= r, spread * query_key, 0.0)
            grown = jnp.exp(down)
            end = down[GROUP - 1 : GROUP]
            tasks.append(
                dict(
                    h=h, g=g, system=system, attend=split(attend), q=grown * q_g, end=jnp.exp(end),
                    right=split(jnp.concatenate([b * values[h][span], (b * grown) * k_g], axis=1)),
                    trailing=split(jnp.exp(end - down) * k_g),
                    inverse=eye - jnp.where(below(1), system, 0.0),
                )
            )
    size = 2
    while size < GROUP:
        mask = below(size)
        for t in tasks:
            t["split"] = split(t["inverse"])
            t["half"] = mm(split(jnp.where(mask, t["system"], 0.0)), t["split"])
        for t in tasks:
            t["inverse"] = t["inverse"] - mm(t["split"], split(t["half"]))
        size *= 2
    for t in tasks:
        t["writes"] = split(mm(split(t["inverse"]), t["right"]))
    for t in tasks:
        seen = mm(t["attend"], t["writes"])
        t["inner"] = seen[:, :DK]
        t["reach"] = t["q"] - seen[:, DK:]
        moved = mm(t["trailing"], t["writes"], 0, 0)
        t["a"] = t["end"] * eye_k - moved[:, DK:]
        t["b"] = moved[:, :DK]
    whole = [None, None]
    for t in tasks:
        h, span = t["h"], slice(t["g"] * GROUP, (t["g"] + 1) * GROUP)
        if t["g"] == 0:
            reach[h, span] = t["reach"] * keep
            inner[h, span] = t["inner"]
            whole[h] = jnp.concatenate([t["a"], t["b"]], axis=1)
        else:
            entering = split(whole[h])
            both = mm(split(t["reach"]), entering)
            reach[h, span] = both[:, :DK] * keep
            inner[h, span] = t["inner"] + both[:, DK:]
            step = mm(split(t["a"]), entering)
            whole[h] = jnp.concatenate([step[:, :DK], step[:, DK:] + t["b"]], axis=1)
    for h in range(2):
        ab[h, :, :DK] = whole[h][:, :DK] * keep
        ab[h, :, DK:] = whole[h][:, DK:]

    for k in range(1, min(2, relays)):
        relay(k)

    def between(k, source, target, device):
        return pltpu.make_async_remote_copy(
            src_ref=source, dst_ref=target, send_sem=sends.at[k], recv_sem=recvs.at[k], device_id=device, device_id_type=MESH
        )

    first = between(0, ab.at[1 - core], blocks.at[core], mate)
    first.start()
    blocks[core] = ab[core]
    first.wait_recv()
    chips[side] = joined(blocks[1], blocks[0])
    second = between(1, chips.at[side], chips.at[side], other)
    second.start()
    second.wait_recv()
    for k in range(2, relays):
        relay(k)

    rise = between(2, total, lower, crown)

    @pl.when((place == 1) | top)
    def _():
        total[...] = joined(chips[1], chips[0])

    @pl.when(place == 1)
    def _():
        rise.start()

    def hop(step, part):
        span = pl.ds(part * rows, rows)
        return pltpu.make_async_remote_copy(
            src_ref=total.at[span] if step == 0 else ring.at[step - 1, span],
            dst_ref=ring.at[step, span],
            send_sem=ring_send.at[step, part],
            recv_sem=ring_recv.at[step, part],
            device_id=onward,
            device_id_type=MESH,
        )

    def pass_on(k, device):
        return pltpu.make_async_remote_copy(
            src_ref=goes, dst_ref=came, send_sem=line_send.at[k], recv_sem=line_recv.at[0], device_id=device, device_id_type=MESH
        )

    def far(k):
        return pass_on(k, at(chip + QUAD * (k + 1), core))

    def given(k, target):
        return between(3 + k, states.at[0 if k < 2 else 1], states.at[0], target)

    @pl.when(top)
    def _():
        rise.wait_recv()
        total[...] = joined(total[...], lower[...])

        @pl.when(upper & (quad < quads - 1))
        def _():
            for part in range(CHUNKS):
                hop(0, part).start()

        for step in range(quads - middle - 1):

            @pl.when(quad - middle > step)
            def _():
                for part in range(CHUNKS):
                    hop(step, part).wait_recv()
                    if step < quads - middle - 2:

                        @pl.when(quad < quads - 1)
                        def _():
                            hop(step + 1, part).start()

                acc[...] = ring[0] if step == 0 else joined(acc[...], ring[step])

        @pl.when(quad == 0)
        def _():
            came[...] = jnp.zeros_like(came)

        @pl.when(quad > 0)
        def _():
            pass_on(0, onward).wait_recv()

        @pl.when(quad < middle)
        def _():
            goes[...] = mm(split(total[:, :DK]), split(came[...])) + total[:, DK:]

        @pl.when(quad < middle - 1)
        def _():
            pass_on(0, onward).start()

        @pl.when(quad == middle - 1)
        def _():
            pl.semaphore_wait(clear, 1)
            for k in reversed(range(quads - middle)):
                far(k).start()

        @pl.when(quad <= middle)
        def _():
            states[0] = came[...]

        @pl.when(quad > middle)
        def _():
            states[0] = mm(split(acc[:, :DK]), split(came[...])) + acc[:, DK:]

        given(0, at(base, core)).start()
        given(1, at(base + 1, core)).start()
        states[1] = mm(split(lower[:, :DK]), split(states[0])) + lower[:, DK:]
        given(2, at(base + 2, core)).start()
        states[2] = mm(split(chips[0, :, :DK]), split(states[1])) + chips[0, :, DK:]

    for k in range(3):

        @pl.when(place == k)
        def _():
            given(k, crown).wait_recv()

    @pl.when((place == 0) | (place == 2))
    def _():
        states[2] = states[0]

    @pl.when(place == 1)
    def _():
        states[2] = mm(split(chips[0, :, :DK]), split(states[0])) + chips[0, :, DK:]

    states[3] = mm(split(blocks[0, :, :DK]), split(states[2])) + blocks[0, :, DK:]
    fifth = between(6, states.at[3 - core], states.at[4], mate)
    fifth.start()

    def read(h, state):
        reads = inner[h] + mm(split(reach[h]), split(state))
        scaled = reads * lax.rsqrt(jnp.mean(reads * reads, axis=-1, keepdims=True) + eps) * gain_ref[...]
        out_ref[:, pl.ds(pl.multiple_of(h * DK, DK), DK)] = scaled.astype(BF16)

    read(core, states[2 + core])
    fifth.wait_recv()
    read(1 - core, states[4])
    for done in (first, second, fifth):
        done.wait_send()

    @pl.when(place == 1)
    def _():
        rise.wait_send()

    @pl.when(top)
    def _():
        for k in range(3):
            given(k, at(base + k, core)).wait_send()

    @pl.when(top & (quad < middle - 1))
    def _():
        pass_on(0, onward).wait_send()

    @pl.when(top & (quad == middle - 1))
    def _():
        for k in range(quads - middle):
            far(k).wait_send()

    for step in range(quads - middle - 1):

        @pl.when(top & (quad < quads - 1) & (quad - middle >= step))
        def _():
            for part in range(CHUNKS):
                hop(step, part).wait_send()
    for copy in sent + passed:
        copy.wait_send()

    @pl.when(me < n - 1)
    def _():
        rim.wait_send()


def per_device(
    hidden,
    w_query,
    w_key,
    payload_projection_matrix,
    conv_weight,
    log_decay,
    beta_rate,
    norm_gain,
    head_order,
    block_starts,
):
    n, heads = lax.axis_size("ctx"), lax.axis_size("head")
    (count, model), shard = hidden.shape, w_query.shape[0]
    half, width = shard // 2, 4 * DK
    quads = n // (2 * QUAD)
    steps = max(quads - quads // 2 - 1, 1)
    hbm = pl.BlockSpec(memory_space=pl.ANY)
    smem, vmem = pl.BlockSpec(memory_space=pltpu.SMEM), pl.BlockSpec(memory_space=pltpu.VMEM)
    dma = pltpu.SemaphoreType.DMA
    pair = pltpu.VMEM((2, DK, 2 * DK), F32)
    one = pltpu.VMEM((DK, 2 * DK), F32)
    state = pltpu.VMEM((DK, DK), F32)
    rows = pltpu.VMEM((2, count, DK), F32)
    return pl.pallas_call(
        functools.partial(kernel, n),
        out_shape=jax.ShapeDtypeStruct((count, 2 * DK), BF16),
        in_specs=[smem, smem] + [hbm] * 4 + [vmem] * 4,
        out_specs=vmem,
        scratch_shapes=[
            pltpu.VMEM((heads, half, DK), BF16),
            pltpu.VMEM((heads, half, DK), BF16),
            pltpu.VMEM((heads, half, 2 * DK), BF16),
            pltpu.VMEM((heads, half, width), BF16),
            pltpu.VMEM((heads * shard, width), BF16),
            pltpu.VMEM((count + RIM, model), BF16),
            pltpu.VMEM((4 * heads, KCONV, DK), F32),
            pltpu.VMEM((count + RIM, width), F32),
            pair, rows, rows,
            pair, pair, one, one, pltpu.VMEM((steps, DK, 2 * DK), F32), one, state, state,
            pltpu.VMEM((5, DK, DK), F32),
            dma((3, heads)), dma((heads,)), dma((heads,)), dma((heads,)), dma((heads,)), dma((2,)), dma((2,)),
            dma((7,)), dma((7,)), dma((steps, CHUNKS)), dma((steps, CHUNKS)), dma((quads - quads // 2,)), dma((1,)),
            pltpu.SemaphoreType.REGULAR,
        ],
        compiler_params=pltpu.CompilerParams(collective_id=0, has_side_effects=True, vmem_limit_bytes=56 << 20),
    )(
        head_order, block_starts, w_query, w_key, payload_projection_matrix, hidden, conv_weight, log_decay, beta_rate,
        norm_gain.reshape(1, DK),
    )


def solution(mesh):
    return jax.shard_map(
        per_device,
        mesh=mesh,
        in_specs=(
            P("ctx", None),
            P("head", None),
            P("head", None),
            P("head", None),
            P(),
            P("head", "ctx"),
            P("head", "ctx"),
            P(),
            P(),
            P("ctx"),
        ),
        out_specs=P("ctx", "head"),
        check_vma=False,
    )
```
